128 devices in a mesh: seq: 16 (over x_hi, z, core), section: 8 (over y, x_lo).
Axes of the slice: x: 4 (x_hi: 2, x_lo: 2; x = x_hi * 2 + x_lo), y: 4, z: 4, core: 2. Of those that a mesh axis runs over, the one named last changes fastest.
Arguments:
- query: bfloat16 [32768, 2048], P(('section', 'seq')), parts along dimension 0, may hold values from -6 to 6
- keys: bfloat16 [32768, 1024], P(('section', 'seq')), parts along dimension 0, may hold values from -6 to 6
- values: bfloat16 [32768, 1024], P(('section', 'seq')), parts along dimension 0, may hold values from -6 to 6
- tail_keys: bfloat16 [32768, 1024], P(('section', 'seq')), parts along dimension 0, may hold values from -6 to 6
- cached_tail_values: bfloat16 [32768, 1024], P(('section', 'seq')), parts along dimension 0, may hold values from -6 to 6
- output_gradient: bfloat16 [32768, 2048], P(('section', 'seq')), parts along dimension 0, may hold values from -6 to 6
- forward_output: bfloat16 [32768, 2048], P(('section', 'seq')), parts along dimension 0, may hold values from -2 to 2
- stretch_index: int32 [1], replicated, may hold values from 0 to 15
- valid_counts: int32 [128], P(('section', 'seq')), parts along dimension 0, may hold values from 0 to 256, as said below
Outputs:
- grad_query: bfloat16 [32768, 2048], P(('section', 'seq')), parts along dimension 0
- grad_keys: bfloat16 [32768, 1024], P(('section', 'seq')), parts along dimension 0
- grad_values: bfloat16 [32768, 1024], P(('section', 'seq')), parts along dimension 0
- grad_tail_keys: bfloat16 [32768, 1024], P(('section', 'seq')), parts along dimension 0
- grad_tail_values: bfloat16 [32768, 1024], P(('section', 'seq')), parts along dimension 0
The draws below stay inside these ranges and needn't reach their ends.
There are 8 independent parts, one for each index of `section`. The reference program is written for one: setup_inputs(seed, part) draws one part's arguments, and reference() takes and returns one part's arrays. A program takes and returns all parts, laid end to end along the dimension named above; an argument that names none is the same for every part. Nothing has to cross between parts.
Inputs may be any that keep to these rules, and one draw needn't show every extreme that they name: `valid_counts`: the valid tokens are a prefix of the stretch: device d's count is min(256, max(0, V - d * 256)) for one total V per draw; the first device is always full and the last always holds none.
All inputs are finite; a program needn't handle non-finite values.
Results may differ from the reference program's by a relative error of at most 0.0058.
Values may be sent and summed in bfloat16 or wider, within the bound.
A program may use at most 192 MiB of HBM per device.

```python
import math
import jax
import jax.numpy as jnp
from jax import lax

WINDOW_TOKENS = 4096
QUERY_HEAD_COUNT = 16
KEY_VALUE_HEADS = 8
HEAD_SIZE = 128
QSCALE = 144
TOK_DEV = 256
N_SEQ = 16


def shared_direction(starting_key):
    selected_rows = jax.random.bernoulli(jax.random.fold_in(starting_key, 101), 0.5, (KEY_VALUE_HEADS, HEAD_SIZE))
    return jnp.where(selected_rows, 1.0, -1.0).astype(jnp.float32)


def softcapped_rows(starting_key, draw_label, count_of_rows, query_group_count):
    direction = shared_direction(starting_key)
    own_key = jax.random.fold_in(starting_key, draw_label)
    complete_shape = (count_of_rows, KEY_VALUE_HEADS, query_group_count, HEAD_SIZE)
    per_head_shape = (count_of_rows, KEY_VALUE_HEADS, query_group_count, 1)
    spread_draw = jax.random.uniform(jax.random.fold_in(own_key, 2), per_head_shape, jnp.float32, 0.0, 1.0)
    jitter = jax.random.normal(jax.random.fold_in(own_key, 1), complete_shape, jnp.float32)
    amplitude = 3.0 * spread_draw * spread_draw
    flips = jax.random.bernoulli(jax.random.fold_in(own_key, 3), 0.5, per_head_shape)
    row_signs = jnp.where(flips, 1.0, -1.0).astype(jnp.float32)
    merged_result = jitter + amplitude * row_signs * direction[None, :, None, :]
    return jnp.clip(merged_result, -6.0, 6.0).reshape(count_of_rows, KEY_VALUE_HEADS * query_group_count * HEAD_SIZE)


def draw_query(key, part):
    return softcapped_rows(key, 7, WINDOW_TOKENS, QUERY_HEAD_COUNT // KEY_VALUE_HEADS).astype(jnp.bfloat16)


def draw_keys(key, part):
    return softcapped_rows(key, 17, WINDOW_TOKENS, 1).astype(jnp.bfloat16)


def draw_tail_keys(key, part):
    return softcapped_rows(key, 29, WINDOW_TOKENS, 1).astype(jnp.bfloat16)


def draw_valid_counts(key, part):
    valid_total = jax.random.randint(jax.random.fold_in(key, 11), (), TOK_DEV, (N_SEQ - 1) * TOK_DEV + 1)
    starts = jnp.arange(N_SEQ, dtype=jnp.int32) * TOK_DEV
    return jnp.clip(valid_total - starts, 0, TOK_DEV).astype(jnp.int32)


def block_scale(rng, dims, pieces, low, largest):
    def one(dim, shards_of):
        heights = jax.random.uniform(jax.random.fold_in(jax.random.fold_in(rng, 6), dim), (shards_of,), jnp.float32, low / len(pieces), largest / len(pieces))
        return jnp.repeat(jnp.exp(heights), dims[dim] // shards_of).reshape((-1,) + (1,) * (len(dims) - dim - 1))

    factor_of = one(*pieces[0])
    for cut in pieces[1:]:
        factor_of = factor_of * one(*cut)
    return factor_of


def gaussian(rng, dims, scale, most, pieces=(), kind=jnp.bfloat16):
    result = scale * jax.random.normal(rng, dims, jnp.float32)
    if pieces:
        result = result * block_scale(rng, dims, pieces, -0.22, 0.18)
    return jnp.clip(result, -most, most).astype(kind)


def setup_inputs(seed: int = 0, part: int = 0) -> dict:
    splits = jax.random.split(jax.random.key(seed), 10)
    part_splits = jax.random.split(jax.random.fold_in(splits[9], part), 10)
    return {
        "query": draw_query(jax.random.fold_in(jax.random.fold_in(splits[9], part), 71), part),
        "keys": draw_keys(jax.random.fold_in(jax.random.fold_in(splits[9], part), 71), part),
        "values": gaussian(part_splits[2], (WINDOW_TOKENS, KEY_VALUE_HEADS * HEAD_SIZE), 1.0, 6.0, ((0, 16),)),
        "tail_keys": draw_tail_keys(jax.random.fold_in(jax.random.fold_in(splits[9], part), 71), part),
        "cached_tail_values": gaussian(part_splits[4], (WINDOW_TOKENS, KEY_VALUE_HEADS * HEAD_SIZE), 1.0, 6.0, ((0, 16),)),
        "output_gradient": gaussian(part_splits[5], (WINDOW_TOKENS, QUERY_HEAD_COUNT * HEAD_SIZE), 1.0, 6.0, ((0, 16),)),
        "forward_output": gaussian(part_splits[6], (WINDOW_TOKENS, QUERY_HEAD_COUNT * HEAD_SIZE), 0.3, 2.0, ((0, 16),)),
        "stretch_index": jax.random.randint(splits[7], (1,), 0, N_SEQ).astype(jnp.int32),
        "valid_counts": draw_valid_counts(jax.random.fold_in(jax.random.fold_in(splits[9], part), 71), part),
    }


softcap = 50.0

def to_bfloat(values_in):
    return lax.optimization_barrier(values_in.astype(jnp.bfloat16)).astype(jnp.float32)

def reference(query, keys, values, tail_keys, cached_tail_values, output_gradient, forward_output, stretch_index, valid_counts):
    rows_per_block = TOK_DEV
    devices = N_SEQ
    window = WINDOW_TOKENS
    head_groups = QUERY_HEAD_COUNT // KEY_VALUE_HEADS
    key_value_width = KEY_VALUE_HEADS * HEAD_SIZE
    window_span = (devices + 1) * rows_per_block
    score_scale = 1.0 / (math.sqrt(QSCALE) * softcap)
    grad_scale = 1.0 / math.sqrt(QSCALE)
    shift_rows = (stretch_index[0] * rows_per_block).astype(jnp.int32)
    tail_key_rows = jnp.roll(tail_keys, -shift_rows, axis=0)
    tail_value_rows = jnp.roll(cached_tail_values, -shift_rows, axis=0)
    extended_keys = jnp.concatenate([tail_key_rows, keys], 0)
    extended_values = jnp.concatenate([tail_value_rows, values], 0)
    positions = jnp.arange(2 * window, dtype=jnp.int32)
    stretch_pos = positions - window
    owner = jnp.clip(stretch_pos // rows_per_block, 0, devices - 1).astype(jnp.int32)
    ext_live = (positions < window) | (stretch_pos % rows_per_block < valid_counts[owner])

    def one_block(ext_grad, index):
        begin_offset = (index * rows_per_block).astype(jnp.int32)
        query_head_rows = lax.dynamic_slice_in_dim(query, begin_offset, rows_per_block, 0).reshape(rows_per_block, KEY_VALUE_HEADS, head_groups, HEAD_SIZE).astype(jnp.float32)
        output_heads = lax.dynamic_slice_in_dim(output_gradient, begin_offset, rows_per_block, 0).reshape(rows_per_block, KEY_VALUE_HEADS, head_groups, HEAD_SIZE).astype(jnp.float32)
        stored_head_output = lax.dynamic_slice_in_dim(forward_output, begin_offset, rows_per_block, 0).reshape(rows_per_block, KEY_VALUE_HEADS, head_groups, HEAD_SIZE).astype(jnp.float32)
        key_window_span = lax.dynamic_slice_in_dim(extended_keys, begin_offset, window_span, 0).reshape(window_span, KEY_VALUE_HEADS, HEAD_SIZE).astype(jnp.float32)
        value_window_span = lax.dynamic_slice_in_dim(extended_values, begin_offset, window_span, 0).reshape(window_span, KEY_VALUE_HEADS, HEAD_SIZE).astype(jnp.float32)
        key_pos = begin_offset + jnp.arange(window_span, dtype=jnp.int32)
        key_live = lax.dynamic_slice_in_dim(ext_live, begin_offset, window_span, 0)
        query_pos = window + begin_offset + jnp.arange(rows_per_block, dtype=jnp.int32)
        query_live = lax.dynamic_slice_in_dim(ext_live, window + begin_offset, rows_per_block, 0)
        mask = (key_pos[None, :] >= query_pos[:, None] - window + 1) & (key_pos[None, :] <= query_pos[:, None])
        mask = mask & key_live[None, :] & query_live[:, None]
        raw = jnp.einsum('qhgd,khd->hgqk', query_head_rows, key_window_span)
        tanh_part = jnp.tanh(raw * score_scale)
        scores = softcap * tanh_part
        total = lax.optimization_barrier(jnp.sum(jnp.where(mask[None, None], jnp.exp(scores), 0.0), axis=3))
        log_total = jnp.log(jnp.where(query_live[None, None, :], total, 1.0))
        prob = jnp.where(mask[None, None], jnp.exp(scores - log_total[..., None]), 0.0)
        delta = jnp.einsum('qhgd,qhgd->hgq', output_heads, stored_head_output)
        prob_grad = jnp.einsum('qhgd,khd->hgqk', output_heads, value_window_span)
        pre_grad = to_bfloat(prob * (prob_grad - delta[..., None]) * (1.0 - tanh_part * tanh_part) * grad_scale)
        prob_low = to_bfloat(prob)
        query_grad = jnp.einsum('hgqk,khd->qhgd', pre_grad, key_window_span).reshape(rows_per_block, QUERY_HEAD_COUNT * HEAD_SIZE)
        key_part = jnp.einsum('hgqk,qhgd->khd', pre_grad, query_head_rows).reshape(devices + 1, rows_per_block, key_value_width)
        value_part = jnp.einsum('hgqk,qhgd->khd', prob_low, output_heads).reshape(devices + 1, rows_per_block, key_value_width)
        block_ids = jnp.arange(devices + 1, dtype=jnp.int32)
        keep = (block_ids == devices)[:, None, None]
        key_part = jnp.where(keep, key_part, to_bfloat(key_part)).reshape(window_span, key_value_width)
        value_part = jnp.where(keep, value_part, to_bfloat(value_part)).reshape(window_span, key_value_width)
        current = lax.dynamic_slice_in_dim(ext_grad, begin_offset, window_span, 1)
        ext_grad = lax.dynamic_update_slice_in_dim(ext_grad, current + jnp.stack([key_part, value_part]), begin_offset, 1)
        return (ext_grad, query_grad.astype(jnp.bfloat16))
    initial = jnp.zeros((2, 2 * window, key_value_width), jnp.float32)
    ext_grad, query_grads = lax.scan(one_block, initial, jnp.arange(devices, dtype=jnp.int32))
    grad_query = query_grads.reshape(window, QUERY_HEAD_COUNT * HEAD_SIZE)
    grad_keys = ext_grad[0, window:].astype(jnp.bfloat16)
    grad_values = ext_grad[1, window:].astype(jnp.bfloat16)
    grad_tail_keys = jnp.roll(ext_grad[0, :window].astype(jnp.bfloat16), shift_rows, axis=0)
    grad_tail_values = jnp.roll(ext_grad[1, :window].astype(jnp.bfloat16), shift_rows, axis=0)
    return (grad_query, grad_keys, grad_values, grad_tail_keys, grad_tail_values)
```

```python
import functools
import math
import jax
import jax.numpy as jnp
from jax import lax
from jax.experimental import pallas as pl
from jax.experimental.pallas import tpu as pltpu
from jax.sharding import PartitionSpec as P

D = 128
BLK = 256
NB = 16
SCALE = 1.0 / (math.sqrt(144) * 50.0)
F32 = jnp.float32
BF = jnp.bfloat16
TQ = 512


def attn_kernel(tq, scal, q_ref, do_ref, dl_ref, kv_ref,
                dq_ref, g_ref,
                ek, ev, gk, gv, p_s, h_s, obuf, sem, osem):
    t = pl.program_id(0)
    nt = pl.num_programs(0)
    c = scal[0]
    total = scal[1]
    nb = tq // BLK
    win = NB * BLK

    @pl.when(t == 0)
    def _():
        copies = []
        for j in range(NB):
            src = lax.rem(j + c, NB)
            copies.append(pltpu.make_async_copy(kv_ref.at[0, pl.ds(src * BLK, BLK), :], ek.at[pl.ds(j * BLK, BLK), :], sem.at[j]))
            copies.append(pltpu.make_async_copy(kv_ref.at[2, pl.ds(src * BLK, BLK), :], ev.at[pl.ds(j * BLK, BLK), :], sem.at[NB + j]))
        copies.append(pltpu.make_async_copy(kv_ref.at[1], ek.at[pl.ds(win, win), :], sem.at[2 * NB]))
        copies.append(pltpu.make_async_copy(kv_ref.at[3], ev.at[pl.ds(win, win), :], sem.at[2 * NB + 1]))
        for cp in copies:
            cp.start()
        gk[...] = jnp.zeros_like(gk)
        gv[...] = jnp.zeros_like(gv)
        for cp in copies:
            cp.wait()

    @pl.when(t * tq < total)
    def _():
        q = q_ref[0]
        do = do_ref[0]
        qt = q.T
        dot = do.T
        dl = dl_ref[0]
        first = t * tq

        def scores(r0):
            return jnp.dot(ek[pl.ds(r0, BLK), :], qt, preferred_element_type=F32)

        def dprob(r0):
            return jnp.dot(ev[pl.ds(r0, BLK), :], dot, preferred_element_type=F32)

        def phase1(slot, raw, dp, tot):
            th = jnp.tanh(raw * SCALE)
            p = jnp.exp(50.0 * th)
            h = p * (1.0 - th * th) * (dp - dl)
            p_s[slot] = p
            h_s[slot] = h
            return tot + p.reshape(BLK // 8, 8, tq).sum(0)

        tot = jnp.zeros((8, tq), F32)
        masks = []
        for j in range(nb):
            row = lax.broadcasted_iota(jnp.int32, (BLK, tq), 0) + j * BLK
            col = lax.broadcasted_iota(jnp.int32, (BLK, tq), 1)
            old = row > col
            ra = pl.multiple_of(first + j * BLK, BLK)
            rb = pl.multiple_of(first + win + j * BLK, BLK)
            raw = jnp.where(old, scores(ra), scores(rb))
            dp = jnp.where(old, dprob(ra), dprob(rb))
            tot = phase1(j, raw, dp, tot)

        def body1(m, tot):
            r0 = pl.multiple_of(first + m * BLK, BLK)
            return phase1(m, scores(r0), dprob(r0), tot)

        tot = lax.fori_loop(nb, NB, body1, tot)
        full = jnp.sum(tot, axis=0, keepdims=True)
        qpos = first + lax.broadcasted_iota(jnp.int32, (1, tq), 1)
        inv = jnp.where(qpos < total, 1.0 / full, 0.0)
        inv12 = inv * (1.0 / 12.0)

        def add(r0, pb, hb, acc):
            gv[pl.ds(r0, BLK), :] += jnp.dot(pb, do, preferred_element_type=F32)
            gk[pl.ds(r0, BLK), :] += jnp.dot(hb, q, preferred_element_type=F32)
            return acc + lax.dot_general(ek[pl.ds(r0, BLK), :], hb, (((0,), (0,)), ((), ())), preferred_element_type=F32)

        acc = jnp.zeros((D, tq), F32)
        for j in range(nb):
            row = lax.broadcasted_iota(jnp.int32, (BLK, tq), 0) + j * BLK
            col = lax.broadcasted_iota(jnp.int32, (BLK, tq), 1)
            old = row > col
            ra = pl.multiple_of(first + j * BLK, BLK)
            rb = pl.multiple_of(first + win + j * BLK, BLK)
            p = p_s[j] * inv
            h = h_s[j] * inv12
            acc = add(ra, jnp.where(old, p, 0.0).astype(BF), jnp.where(old, h, 0.0).astype(BF), acc)
            acc = add(rb, jnp.where(old, 0.0, p).astype(BF), jnp.where(old, 0.0, h).astype(BF), acc)

        def body2(m, acc):
            r0 = pl.multiple_of(first + m * BLK, BLK)
            return add(r0, (p_s[m] * inv).astype(BF), (h_s[m] * inv12).astype(BF), acc)

        acc = lax.fori_loop(nb, NB, body2, acc)
        dq_ref[...] = acc.T.astype(BF)

    @pl.when(t * tq >= total)
    def _():
        dq_ref[...] = jnp.zeros_like(dq_ref)

    @pl.when(t == nt - 1)
    def _():
        outs = []
        obuf[0] = gk[...].astype(BF)
        obuf[1] = gv[...].astype(BF)
        for j in range(NB):
            dst = lax.rem(j + c, NB)
            outs.append(pltpu.make_async_copy(obuf.at[0, pl.ds(j * BLK, BLK), :], g_ref.at[0, 0, pl.ds(dst * BLK, BLK), :], osem.at[j]))
            outs.append(pltpu.make_async_copy(obuf.at[1, pl.ds(j * BLK, BLK), :], g_ref.at[1, 0, pl.ds(dst * BLK, BLK), :], osem.at[NB + j]))
        outs.append(pltpu.make_async_copy(obuf.at[0, pl.ds(win, win), :], g_ref.at[0, 1], osem.at[2 * NB]))
        outs.append(pltpu.make_async_copy(obuf.at[1, pl.ds(win, win), :], g_ref.at[1, 1], osem.at[2 * NB + 1]))
        for cp in outs:
            cp.start()
        for cp in outs:
            cp.wait()


def attn(scal, qd, dl, kv, tq=512):
    n = qd.shape[1]
    any_ = pl.BlockSpec(memory_space=pl.ANY)
    win = NB * BLK
    return pl.pallas_call(
        functools.partial(attn_kernel, tq),
        grid_spec=pltpu.PrefetchScalarGridSpec(
            num_scalar_prefetch=1, grid=(n // tq,),
            in_specs=[pl.BlockSpec((1, tq, D), lambda i, s: (0, i, 0)),
                      pl.BlockSpec((1, tq, D), lambda i, s: (1, i, 0)),
                      pl.BlockSpec((1, 1, tq), lambda i, s: (i, 0, 0)),
                      any_],
            out_specs=[pl.BlockSpec((tq, D), lambda i, s: (i, 0)), any_],
            scratch_shapes=[pltpu.VMEM((2 * win, D), BF), pltpu.VMEM((2 * win, D), BF),
                            pltpu.VMEM((2 * win, D), F32), pltpu.VMEM((2 * win, D), F32),
                            pltpu.VMEM((NB, BLK, tq), F32), pltpu.VMEM((NB, BLK, tq), F32),
                            pltpu.VMEM((2, 2 * win, D), BF),
                            pltpu.SemaphoreType.DMA((2 * NB + 2,)), pltpu.SemaphoreType.DMA((2 * NB + 2,))]),
        out_shape=[jax.ShapeDtypeStruct((n, D), BF), jax.ShapeDtypeStruct((2, 2, n, D), BF)],
        compiler_params=pltpu.CompilerParams(vmem_limit_bytes=60 << 20),
    )(scal, qd, qd, dl, kv)


MESH = pl.DeviceIdType.MESH


def to(peer):
    return {"seq": peer}


def wait_bytes(view, sem):
    pltpu.make_async_copy(view, view, sem).wait()


def entry_barrier(me):
    barrier = pltpu.get_barrier_semaphore()

    def greet(step, carry):
        pl.semaphore_signal(
            barrier, inc=1, device_id=to(lax.rem(me + step, NB)), device_id_type=MESH
        )
        return carry

    lax.fori_loop(1, NB, greet, 0)
    pl.semaphore_wait(barrier, NB - 1)


def cols(index):
    return pl.ds(pl.multiple_of(index * D, D), D)


def rows(index):
    return pl.ds(pl.multiple_of(index * BLK, BLK), BLK)


def scatter_heads(
    q_ref, do_ref, dl_ref, k_ref, v_ref, tk_ref, tv_ref,
    qd_ref, dlg_ref, kv_ref,
    send_q, send_l, send_kv, send_rel, recv_q, recv_l, recv_kv, recv_rel, local,
):
    me = lax.axis_index("seq")
    chip = me // 2
    core = lax.rem(me, 2)
    partner = chip * 2 + 1 - core
    sources = (tk_ref, k_ref, tv_ref, v_ref)
    chips = NB // 2
    own = []
    for a, src in enumerate(sources):
        own.append(pltpu.make_async_copy(src.at[:, cols(chip)], kv_ref.at[a, rows(me)], local.at[a]))
    own.append(pltpu.make_async_copy(q_ref.at[:, cols(me)], qd_ref.at[0, rows(me)], local.at[4]))
    own.append(pltpu.make_async_copy(do_ref.at[:, cols(me)], qd_ref.at[1, rows(me)], local.at[5]))
    own.append(pltpu.make_async_copy(dl_ref.at[me], dlg_ref.at[me], local.at[6]))
    for copy in own:
        copy.start()
    entry_barrier(me)

    def send_chip(step, carry):
        other = lax.rem(chip + step, chips)
        for a, src in enumerate(sources):
            pltpu.make_async_remote_copy(
                src_ref=src.at[:, cols(other)], dst_ref=kv_ref.at[a, rows(me)],
                send_sem=send_kv.at[other], recv_sem=recv_kv.at[chip],
                device_id=to(other * 2 + core), device_id_type=MESH,
            ).start()
        return carry

    lax.fori_loop(1, chips, send_chip, 0)
    for a, src in enumerate(sources):
        pltpu.make_async_remote_copy(
            src_ref=src.at[:, cols(chip)], dst_ref=kv_ref.at[a, rows(me)],
            send_sem=send_rel.at[chip], recv_sem=recv_rel.at[chip],
            device_id=to(partner), device_id_type=MESH,
        ).start()

    def send_peer(step, carry):
        peer = lax.rem(me + step, NB)
        for a, src in enumerate((q_ref, do_ref)):
            pltpu.make_async_remote_copy(
                src_ref=src.at[:, cols(peer)], dst_ref=qd_ref.at[a, rows(me)],
                send_sem=send_q.at[peer], recv_sem=recv_q.at[me],
                device_id=to(peer), device_id_type=MESH,
            ).start()
        pltpu.make_async_remote_copy(
            src_ref=dl_ref.at[peer], dst_ref=dlg_ref.at[me],
            send_sem=send_l.at[peer], recv_sem=recv_l.at[me],
            device_id=to(peer), device_id_type=MESH,
        ).start()
        return carry

    lax.fori_loop(1, NB, send_peer, 0)

    def relay(step, carry):
        other = lax.rem(chip + chips - step, chips)
        view = kv_ref.at[:, rows(other * 2 + core)]
        wait_bytes(view, recv_kv.at[other])
        pltpu.make_async_remote_copy(
            src_ref=view, dst_ref=view,
            send_sem=send_rel.at[other], recv_sem=recv_rel.at[other],
            device_id=to(partner), device_id_type=MESH,
        ).start()
        return carry

    lax.fori_loop(1, chips, relay, 0)

    def finish_peer(step, carry):
        peer = lax.rem(me + step, NB)
        wait_bytes(qd_ref.at[:, rows(peer)], recv_q.at[peer])
        wait_bytes(dlg_ref.at[peer], recv_l.at[peer])
        wait_bytes(qd_ref.at[:, rows(peer)], send_q.at[peer])
        wait_bytes(dlg_ref.at[peer], send_l.at[peer])
        return carry

    lax.fori_loop(1, NB, finish_peer, 0)

    def finish_chip(step, carry):
        other = lax.rem(chip + step, chips)
        wait_bytes(kv_ref.at[:, rows(other * 2 + 1 - core)], recv_rel.at[other])
        wait_bytes(kv_ref.at[:, rows(other * 2 + core)], send_rel.at[other])
        return carry

    lax.fori_loop(0, chips, finish_chip, 0)

    def finish_send(step, carry):
        other = lax.rem(chip + step, chips)
        wait_bytes(kv_ref.at[:, rows(other * 2 + core)], send_kv.at[other])
        return carry

    lax.fori_loop(1, chips, finish_send, 0)
    for copy in own:
        copy.wait()


def gather_heads(q, do, dl, k, v, tk, tv):
    any_ = pl.BlockSpec(memory_space=pl.ANY)
    dma = pltpu.SemaphoreType.DMA
    return pl.pallas_call(
        scatter_heads,
        in_specs=[any_] * 7,
        out_specs=[any_] * 3,
        out_shape=[
            jax.ShapeDtypeStruct((2, NB * BLK, D), BF),
            jax.ShapeDtypeStruct(dl.shape, F32),
            jax.ShapeDtypeStruct((4, NB * BLK, D), BF),
        ],
        scratch_shapes=[
            dma((NB,)), dma((NB,)), dma((NB // 2,)), dma((NB // 2,)),
            dma((NB,)), dma((NB,)), dma((NB // 2,)), dma((NB // 2,)), dma((7,)),
        ],
        compiler_params=pltpu.CompilerParams(collective_id=0, has_side_effects=True),
    )(q, do, dl, k, v, tk, tv)


def return_heads(
    dq_ref, g_ref, gq_ref, gkv_ref,
    mine, theirs, both, send_q, recv_q, send_g, recv_g, send_x, recv_x, local,
):
    me = lax.axis_index("seq")
    chip = me // 2
    core = lax.rem(me, 2)
    partner = chip * 2 + 1 - core
    own = pltpu.make_async_copy(dq_ref.at[rows(me)], gq_ref.at[:, cols(me)], local.at[0])
    fetch = pltpu.make_async_copy(g_ref.at[core], mine, local.at[1])
    own.start()
    fetch.start()
    entry_barrier(me)
    part = 4
    span = NB * BLK // part

    def give(step, carry):
        piece = pl.ds(pl.multiple_of(step * span, span), span)
        pltpu.make_async_remote_copy(
            src_ref=g_ref.at[1 - core, :, piece], dst_ref=theirs.at[:, piece],
            send_sem=send_x.at[step], recv_sem=recv_x.at[step],
            device_id=to(partner), device_id_type=MESH,
        ).start()
        return carry

    lax.fori_loop(0, part, give, 0)

    def send_peer(step, carry):
        peer = lax.rem(me + step, NB)
        pltpu.make_async_remote_copy(
            src_ref=dq_ref.at[rows(peer)], dst_ref=gq_ref.at[:, cols(me)],
            send_sem=send_q.at[peer], recv_sem=recv_q.at[me],
            device_id=to(peer), device_id_type=MESH,
        ).start()
        return carry

    lax.fori_loop(1, NB, send_peer, 0)
    fetch.wait()

    def combine(step, carry):
        piece = pl.ds(pl.multiple_of(step * span, span), span)
        wait_bytes(theirs.at[:, piece], recv_x.at[step])
        both[:, piece, :] = (mine[:, piece, :].astype(F32) + theirs[:, piece, :].astype(F32)).astype(BF)

        def send_block(index, inner):
            peer = step * (NB // part) + index

            @pl.when(peer != me)
            def _():
                pltpu.make_async_remote_copy(
                    src_ref=both.at[:, rows(peer)], dst_ref=gkv_ref.at[core, :, :, cols(chip)],
                    send_sem=send_g.at[peer], recv_sem=recv_g.at[me],
                    device_id=to(peer), device_id_type=MESH,
                ).start()

            return inner

        lax.fori_loop(0, NB // part, send_block, 0)
        return carry

    lax.fori_loop(0, part, combine, 0)
    last = pltpu.make_async_copy(both.at[:, rows(me)], gkv_ref.at[core, :, :, cols(chip)], local.at[2])
    last.start()

    def finish(step, carry):
        peer = lax.rem(me + step, NB)
        wait_bytes(dq_ref.at[rows(peer)], recv_q.at[peer])
        wait_bytes(dq_ref.at[rows(peer)], send_q.at[peer])
        wait_bytes(both.at[:, rows(peer)], recv_g.at[peer])
        wait_bytes(both.at[:, rows(peer)], send_g.at[peer])
        return carry

    lax.fori_loop(1, NB, finish, 0)

    def finish_x(step, carry):
        piece = pl.ds(pl.multiple_of(step * span, span), span)
        wait_bytes(theirs.at[:, piece], send_x.at[step])
        return carry

    lax.fori_loop(0, part, finish_x, 0)
    own.wait()
    last.wait()


def scatter_grads(dq, g):
    any_ = pl.BlockSpec(memory_space=pl.ANY)
    dma = pltpu.SemaphoreType.DMA
    vm = pltpu.VMEM((2, NB * BLK, D), BF)
    return pl.pallas_call(
        return_heads,
        in_specs=[any_] * 2,
        out_specs=[any_] * 2,
        out_shape=[
            jax.ShapeDtypeStruct((BLK, NB * D), BF),
            jax.ShapeDtypeStruct((2, 2, BLK, NB // 2 * D), BF),
        ],
        scratch_shapes=[vm, vm, vm, dma((NB,)), dma((NB,)), dma((NB,)), dma((NB,)), dma((4,)), dma((4,)), dma((3,))],
        compiler_params=pltpu.CompilerParams(collective_id=1, has_side_effects=True),
    )(dq, g)


def per_device(query, keys, values, tail_keys, cached_tail_values, output_gradient, forward_output, stretch_index, valid_counts):
    delta = jnp.sum(
        (output_gradient.astype(F32) * forward_output.astype(F32)).reshape(BLK, NB, D), axis=2
    )
    count = jnp.full((NB, D), valid_counts[0].astype(F32))
    extra = jnp.concatenate([delta.T, count], axis=1)[:, None, :]
    qd, extras, kv = gather_heads(query, output_gradient, extra, keys, values, tail_keys, cached_tail_values)
    live = jnp.sum(extras[:, 0, BLK]).astype(jnp.int32)
    scal = jnp.stack([stretch_index[0], live])
    dl = extras[:, 0, :BLK].reshape(-1, 1, TQ)
    dq, g = attn(scal, qd, dl, kv)
    gq, gkv = scatter_grads(dq, g)
    return gq, gkv[0, 1], gkv[1, 1], gkv[0, 0], gkv[1, 0]


def solution(mesh):
    tokens = P(("section", "seq"), None)
    return jax.shard_map(
        per_device,
        mesh=mesh,
        in_specs=(tokens,) * 7 + (P(), P(("section", "seq"))),
        out_specs=(tokens,) * 5,
        check_vma=False,
    )
```

```python
import functools
import math
import jax
import jax.numpy as jnp
from jax import lax
from jax.experimental import pallas as pl
from jax.experimental.pallas import tpu as pltpu
from jax.sharding import PartitionSpec as P

D = 128
BLK = 256
NB = 16
SCALE = 1.0 / (math.sqrt(144) * 50.0)
EXPO = 50.0 * math.log2(math.e)
F32 = jnp.float32
BF = jnp.bfloat16
WIN = NB * BLK
TQ = 512


def attn_kernel(tq, sub, kb, kb2, norm, vacc, scal, q_ref, do_ref, dl_ref, kv_ref,
                dq_ref, g_ref,
                ek, ev, gk, gv, p_s, h_s, wq, wd, dacc, obuf, sem, osem):
    t = pl.program_id(0)
    nt = pl.num_programs(0)
    c = scal[0]
    total = scal[1]

    @pl.when(t == 0)
    def _():
        copies = []
        for j in range(NB):
            src = lax.rem(j + c, NB)
            copies.append(pltpu.make_async_copy(kv_ref.at[0, pl.ds(src * BLK, BLK), :], ek.at[pl.ds(j * BLK, BLK), :], sem.at[j]))
            copies.append(pltpu.make_async_copy(kv_ref.at[2, pl.ds(src * BLK, BLK), :], ev.at[pl.ds(j * BLK, BLK), :], sem.at[NB + j]))
        copies.append(pltpu.make_async_copy(kv_ref.at[1], ek.at[pl.ds(WIN, WIN), :], sem.at[2 * NB]))
        copies.append(pltpu.make_async_copy(kv_ref.at[3], ev.at[pl.ds(WIN, WIN), :], sem.at[2 * NB + 1]))
        for cp in copies:
            cp.start()
        gk[...] = jnp.zeros_like(gk)
        gv[...] = jnp.zeros_like(gv)
        for cp in copies:
            cp.wait()

    @pl.when(t * tq < total)
    def _():
        first = t * tq
        dl = dl_ref[0]
        q = q_ref[0]
        do = do_ref[0]
        wq[0:D, :] = q.T
        wd[0:D, :] = do.T

        def scores(r0, n):
            return jnp.dot(ek[pl.ds(r0, n), :], wq[0:D, :], preferred_element_type=F32) * SCALE

        def dprob(r0, n):
            return jnp.dot(ev[pl.ds(r0, n), :], wd[0:D, :], preferred_element_type=F32) - dl

        def phase1(at, x, dp):
            n = x.shape[0]
            th = jnp.tanh(x)
            p = jnp.exp2(EXPO * th)
            h = p * (1.0 - th * th) * dp
            p_s[at, :] = p.astype(p_s.dtype)
            h_s[at, :] = h.astype(h_s.dtype)
            return p.reshape(n // 8, 8, tq).sum(0)

        tot = jnp.zeros((8, tq), F32)

        ms = 256

        def mask(s):
            row = lax.broadcasted_iota(jnp.int32, (ms, tq), 0) + s * ms
            col = lax.broadcasted_iota(jnp.int32, (ms, tq), 1)
            return row > col

        for s in range(tq // ms):
            old = mask(s)
            ra = pl.multiple_of(first + s * ms, ms)
            rb = pl.multiple_of(first + WIN + s * ms, ms)
            x = jnp.where(old, scores(ra, ms), scores(rb, ms))
            dp = jnp.where(old, dprob(ra, ms), dprob(rb, ms))
            tot = tot + phase1(pl.ds(s * ms, ms), x, dp)

        def body1(m, tot):
            r0 = pl.multiple_of(first + tq + m * kb, 128)
            for s in range(kb // sub):
                tot = tot + phase1(pl.ds(pl.multiple_of(tq + m * kb + s * sub, 128), sub), scores(r0 + s * sub, sub), dprob(r0 + s * sub, sub))
            return tot

        tot = lax.fori_loop(0, (WIN - tq) // kb, body1, tot)
        full = jnp.sum(tot, axis=0, keepdims=True)
        qpos = first + lax.broadcasted_iota(jnp.int32, (1, tq), 1)
        inv = jnp.where(qpos < total, 1.0 / full, 0.0)
        inv12 = inv * (1.0 / 12.0)
        if not norm:
            col_inv = jnp.broadcast_to(inv, (D, tq)).T
            do = (do.astype(F32) * col_inv).astype(BF)
            q = (q.astype(F32) * (col_inv * (1.0 / 12.0))).astype(BF)

        def ld(at):
            p = p_s[at, :]
            h = h_s[at, :]
            if norm:
                p = p * inv
                h = h * inv12
            return p, h

        def add(r0, n, pb, hb):
            pb = pb.astype(BF)
            hb = hb.astype(BF)
            gv[pl.ds(r0, n), :] += jnp.dot(pb, do, preferred_element_type=F32)
            gk[pl.ds(r0, n), :] += jnp.dot(hb, q, preferred_element_type=F32)
            return lax.dot_general(ek[pl.ds(r0, n), :], hb, (((0,), (0,)), ((), ())), preferred_element_type=F32)

        mk = min(512, tq)
        acc = jnp.zeros((D, tq), F32)
        for s in range(tq // mk):
            row = lax.broadcasted_iota(jnp.int32, (mk, tq), 0) + s * mk
            col = lax.broadcasted_iota(jnp.int32, (mk, tq), 1)
            old = row > col
            ra = pl.multiple_of(first + s * mk, mk)
            rb = pl.multiple_of(first + WIN + s * mk, mk)
            p, h = ld(pl.ds(s * mk, mk))
            z = jnp.zeros_like(p)
            acc = acc + add(ra, mk, jnp.where(old, p, z), jnp.where(old, h, z))
            acc = acc + add(rb, mk, jnp.where(old, z, p), jnp.where(old, z, h))
        if vacc:
            dacc[...] = acc
            acc = 0

        def body2(m, acc):
            r0 = pl.multiple_of(first + tq + m * kb2, 128)
            p, h = ld(pl.ds(pl.multiple_of(tq + m * kb2, 128), kb2))
            d = add(r0, kb2, p, h)
            if vacc:
                dacc[...] += d
                return acc
            return acc + d

        acc = lax.fori_loop(0, (WIN - tq) // kb2, body2, acc)
        if vacc:
            acc = dacc[...]
        if not norm:
            acc = acc * inv12
        dq_ref[...] = acc.T.astype(BF)

    @pl.when(t * tq >= total)
    def _():
        dq_ref[...] = jnp.zeros_like(dq_ref)

    @pl.when(t == nt - 1)
    def _():
        outs = []
        obuf[0] = gk[...].astype(BF)
        obuf[1] = gv[...].astype(BF)
        for j in range(NB):
            dst = lax.rem(j + c, NB)
            outs.append(pltpu.make_async_copy(obuf.at[0, pl.ds(j * BLK, BLK), :], g_ref.at[0, 0, pl.ds(dst * BLK, BLK), :], osem.at[j]))
            outs.append(pltpu.make_async_copy(obuf.at[1, pl.ds(j * BLK, BLK), :], g_ref.at[1, 0, pl.ds(dst * BLK, BLK), :], osem.at[NB + j]))
        outs.append(pltpu.make_async_copy(obuf.at[0, pl.ds(WIN, WIN), :], g_ref.at[0, 1], osem.at[2 * NB]))
        outs.append(pltpu.make_async_copy(obuf.at[1, pl.ds(WIN, WIN), :], g_ref.at[1, 1], osem.at[2 * NB + 1]))
        for cp in outs:
            cp.start()
        for cp in outs:
            cp.wait()


def attn(scal, qd, dl, kv, tq=512, sub=256, kb=1792, kb2=1792, norm=True, vacc=False):
    n = qd.shape[1]
    any_ = pl.BlockSpec(memory_space=pl.ANY)
    dma = pltpu.SemaphoreType.DMA
    return pl.pallas_call(
        functools.partial(attn_kernel, tq, sub, kb, kb2, norm, vacc),
        grid_spec=pltpu.PrefetchScalarGridSpec(
            num_scalar_prefetch=1, grid=(n // tq,),
            in_specs=[pl.BlockSpec((1, tq, D), lambda i, s: (0, i, 0)),
                      pl.BlockSpec((1, tq, D), lambda i, s: (1, i, 0)),
                      pl.BlockSpec((1, 1, tq), lambda i, s: (i, 0, 0)),
                      any_],
            out_specs=[pl.BlockSpec((tq, D), lambda i, s: (i, 0)), any_],
            scratch_shapes=[pltpu.VMEM((2 * WIN, D), BF), pltpu.VMEM((2 * WIN, D), BF),
                            pltpu.VMEM((2 * WIN, D), F32), pltpu.VMEM((2 * WIN, D), F32),
                            pltpu.VMEM((WIN, tq), F32 if norm else BF), pltpu.VMEM((WIN, tq), F32 if norm else BF),
                            pltpu.VMEM((2 * D, tq), BF), pltpu.VMEM((2 * D, tq), BF), pltpu.VMEM((D, tq), F32),
                            pltpu.VMEM((2, 2 * WIN, D), BF),
                            dma((2 * NB + 2,)), dma((2 * NB + 2,))]),
        out_shape=[jax.ShapeDtypeStruct((n, D), BF), jax.ShapeDtypeStruct((2, 2, n, D), BF)],
        compiler_params=pltpu.CompilerParams(vmem_limit_bytes=63 << 20),
    )(scal, qd, qd, dl, kv)


MESH = pl.DeviceIdType.MESH


def to(peer):
    return {"seq": peer}


def wait_bytes(view, sem):
    pltpu.make_async_copy(view, view, sem).wait()


def entry_barrier(me):
    barrier = pltpu.get_barrier_semaphore()

    def greet(step, carry):
        pl.semaphore_signal(
            barrier, inc=1, device_id=to(lax.rem(me + step, NB)), device_id_type=MESH
        )
        return carry

    lax.fori_loop(1, NB, greet, 0)
    pl.semaphore_wait(barrier, NB - 1)


def cols(index):
    return pl.ds(pl.multiple_of(index * D, D), D)


def rows(index):
    return pl.ds(pl.multiple_of(index * BLK, BLK), BLK)


def scatter_heads(
    q_ref, do_ref, dl_ref, k_ref, v_ref, tk_ref, tv_ref,
    qd_ref, dlg_ref, kv_ref,
    send_q, send_l, send_kv, send_rel, recv_q, recv_l, recv_kv, recv_rel, local,
):
    me = lax.axis_index("seq")
    chip = me // 2
    core = lax.rem(me, 2)
    partner = chip * 2 + 1 - core
    sources = (tk_ref, k_ref, tv_ref, v_ref)
    chips = NB // 2
    own = []
    for a, src in enumerate(sources):
        own.append(pltpu.make_async_copy(src.at[:, cols(chip)], kv_ref.at[a, rows(me)], local.at[a]))
    own.append(pltpu.make_async_copy(q_ref.at[:, cols(me)], qd_ref.at[0, rows(me)], local.at[4]))
    own.append(pltpu.make_async_copy(do_ref.at[:, cols(me)], qd_ref.at[1, rows(me)], local.at[5]))
    own.append(pltpu.make_async_copy(dl_ref.at[me], dlg_ref.at[me], local.at[6]))
    for copy in own:
        copy.start()
    entry_barrier(me)

    def send_chip(step, carry):
        other = lax.rem(chip + step, chips)
        for a, src in enumerate(sources):
            pltpu.make_async_remote_copy(
                src_ref=src.at[:, cols(other)], dst_ref=kv_ref.at[a, rows(me)],
                send_sem=send_kv.at[other], recv_sem=recv_kv.at[chip],
                device_id=to(other * 2 + core), device_id_type=MESH,
            ).start()
        return carry

    lax.fori_loop(1, chips, send_chip, 0)
    for a, src in enumerate(sources):
        pltpu.make_async_remote_copy(
            src_ref=src.at[:, cols(chip)], dst_ref=kv_ref.at[a, rows(me)],
            send_sem=send_rel.at[chip], recv_sem=recv_rel.at[chip],
            device_id=to(partner), device_id_type=MESH,
        ).start()

    def send_peer(step, carry):
        peer = lax.rem(me + step, NB)
        for a, src in enumerate((q_ref, do_ref)):
            pltpu.make_async_remote_copy(
                src_ref=src.at[:, cols(peer)], dst_ref=qd_ref.at[a, rows(me)],
                send_sem=send_q.at[peer], recv_sem=recv_q.at[me],
                device_id=to(peer), device_id_type=MESH,
            ).start()
        pltpu.make_async_remote_copy(
            src_ref=dl_ref.at[peer], dst_ref=dlg_ref.at[me],
            send_sem=send_l.at[peer], recv_sem=recv_l.at[me],
            device_id=to(peer), device_id_type=MESH,
        ).start()
        return carry

    lax.fori_loop(1, NB, send_peer, 0)

    def relay(step, carry):
        other = lax.rem(chip + chips - step, chips)
        view = kv_ref.at[:, rows(other * 2 + core)]
        wait_bytes(view, recv_kv.at[other])
        pltpu.make_async_remote_copy(
            src_ref=view, dst_ref=view,
            send_sem=send_rel.at[other], recv_sem=recv_rel.at[other],
            device_id=to(partner), device_id_type=MESH,
        ).start()
        return carry

    lax.fori_loop(1, chips, relay, 0)

    def finish_peer(step, carry):
        peer = lax.rem(me + step, NB)
        wait_bytes(qd_ref.at[:, rows(peer)], recv_q.at[peer])
        wait_bytes(dlg_ref.at[peer], recv_l.at[peer])
        wait_bytes(qd_ref.at[:, rows(peer)], send_q.at[peer])
        wait_bytes(dlg_ref.at[peer], send_l.at[peer])
        return carry

    lax.fori_loop(1, NB, finish_peer, 0)

    def finish_chip(step, carry):
        other = lax.rem(chip + step, chips)
        wait_bytes(kv_ref.at[:, rows(other * 2 + 1 - core)], recv_rel.at[other])
        wait_bytes(kv_ref.at[:, rows(other * 2 + core)], send_rel.at[other])
        return carry

    lax.fori_loop(0, chips, finish_chip, 0)

    def finish_send(step, carry):
        other = lax.rem(chip + step, chips)
        wait_bytes(kv_ref.at[:, rows(other * 2 + core)], send_kv.at[other])
        return carry

    lax.fori_loop(1, chips, finish_send, 0)
    for copy in own:
        copy.wait()


def gather_heads(q, do, dl, k, v, tk, tv):
    any_ = pl.BlockSpec(memory_space=pl.ANY)
    dma = pltpu.SemaphoreType.DMA
    return pl.pallas_call(
        scatter_heads,
        in_specs=[any_] * 7,
        out_specs=[any_] * 3,
        out_shape=[
            jax.ShapeDtypeStruct((2, NB * BLK, D), BF),
            jax.ShapeDtypeStruct(dl.shape, F32),
            jax.ShapeDtypeStruct((4, NB * BLK, D), BF),
        ],
        scratch_shapes=[
            dma((NB,)), dma((NB,)), dma((NB // 2,)), dma((NB // 2,)),
            dma((NB,)), dma((NB,)), dma((NB // 2,)), dma((NB // 2,)), dma((7,)),
        ],
        compiler_params=pltpu.CompilerParams(collective_id=0, has_side_effects=True),
    )(q, do, dl, k, v, tk, tv)


def return_heads(
    dq_ref, g_ref, gq_ref, gkv_ref,
    mine, theirs, both, send_q, recv_q, send_g, recv_g, send_x, recv_x, local,
):
    me = lax.axis_index("seq")
    chip = me // 2
    core = lax.rem(me, 2)
    partner = chip * 2 + 1 - core
    own = pltpu.make_async_copy(dq_ref.at[rows(me)], gq_ref.at[:, cols(me)], local.at[0])
    fetch = pltpu.make_async_copy(g_ref.at[core], mine, local.at[1])
    own.start()
    fetch.start()
    entry_barrier(me)
    part = 4
    span = NB * BLK // part

    def give(step, carry):
        piece = pl.ds(pl.multiple_of(step * span, span), span)
        pltpu.make_async_remote_copy(
            src_ref=g_ref.at[1 - core, :, piece], dst_ref=theirs.at[:, piece],
            send_sem=send_x.at[step], recv_sem=recv_x.at[step],
            device_id=to(partner), device_id_type=MESH,
        ).start()
        return carry

    lax.fori_loop(0, part, give, 0)

    def send_peer(step, carry):
        peer = lax.rem(me + step, NB)
        pltpu.make_async_remote_copy(
            src_ref=dq_ref.at[rows(peer)], dst_ref=gq_ref.at[:, cols(me)],
            send_sem=send_q.at[peer], recv_sem=recv_q.at[me],
            device_id=to(peer), device_id_type=MESH,
        ).start()
        return carry

    lax.fori_loop(1, NB, send_peer, 0)
    fetch.wait()

    def combine(step, carry):
        piece = pl.ds(pl.multiple_of(step * span, span), span)
        wait_bytes(theirs.at[:, piece], recv_x.at[step])
        both[:, piece, :] = (mine[:, piece, :].astype(F32) + theirs[:, piece, :].astype(F32)).astype(BF)

        def send_block(index, inner):
            peer = step * (NB // part) + index

            @pl.when(peer != me)
            def _():
                pltpu.make_async_remote_copy(
                    src_ref=both.at[:, rows(peer)], dst_ref=gkv_ref.at[core, :, :, cols(chip)],
                    send_sem=send_g.at[peer], recv_sem=recv_g.at[me],
                    device_id=to(peer), device_id_type=MESH,
                ).start()

            return inner

        lax.fori_loop(0, NB // part, send_block, 0)
        return carry

    lax.fori_loop(0, part, combine, 0)
    last = pltpu.make_async_copy(both.at[:, rows(me)], gkv_ref.at[core, :, :, cols(chip)], local.at[2])
    last.start()

    def finish(step, carry):
        peer = lax.rem(me + step, NB)
        wait_bytes(dq_ref.at[rows(peer)], recv_q.at[peer])
        wait_bytes(dq_ref.at[rows(peer)], send_q.at[peer])
        wait_bytes(both.at[:, rows(peer)], recv_g.at[peer])
        wait_bytes(both.at[:, rows(peer)], send_g.at[peer])
        return carry

    lax.fori_loop(1, NB, finish, 0)

    def finish_x(step, carry):
        piece = pl.ds(pl.multiple_of(step * span, span), span)
        wait_bytes(theirs.at[:, piece], send_x.at[step])
        return carry

    lax.fori_loop(0, part, finish_x, 0)
    own.wait()
    last.wait()


def scatter_grads(dq, g):
    any_ = pl.BlockSpec(memory_space=pl.ANY)
    dma = pltpu.SemaphoreType.DMA
    vm = pltpu.VMEM((2, NB * BLK, D), BF)
    return pl.pallas_call(
        return_heads,
        in_specs=[any_] * 2,
        out_specs=[any_] * 2,
        out_shape=[
            jax.ShapeDtypeStruct((BLK, NB * D), BF),
            jax.ShapeDtypeStruct((2, 2, BLK, NB // 2 * D), BF),
        ],
        scratch_shapes=[vm, vm, vm, dma((NB,)), dma((NB,)), dma((NB,)), dma((NB,)), dma((4,)), dma((4,)), dma((3,))],
        compiler_params=pltpu.CompilerParams(collective_id=1, has_side_effects=True),
    )(dq, g)


def per_device(query, keys, values, tail_keys, cached_tail_values, output_gradient, forward_output, stretch_index, valid_counts):
    delta = jnp.sum(
        (output_gradient.astype(F32) * forward_output.astype(F32)).reshape(BLK, NB, D), axis=2
    )
    count = jnp.full((NB, D), valid_counts[0].astype(F32))
    extra = jnp.concatenate([delta.T, count], axis=1)[:, None, :]
    qd, extras, kv = gather_heads(query, output_gradient, extra, keys, values, tail_keys, cached_tail_values)
    live = jnp.sum(extras[:, 0, BLK]).astype(jnp.int32)
    scal = jnp.stack([stretch_index[0], live])
    dl = extras[:, 0, :BLK].reshape(-1, 1, TQ)
    dq, g = attn(scal, qd, dl, kv)
    gq, gkv = scatter_grads(dq, g)
    return gq, gkv[0, 1], gkv[1, 1], gkv[0, 0], gkv[1, 0]


def solution(mesh):
    tokens = P(("section", "seq"), None)
    return jax.shard_map(
        per_device,
        mesh=mesh,
        in_specs=(tokens,) * 7 + (P(), P(("section", "seq"))),
        out_specs=(tokens,) * 5,
        check_vma=False,
    )
```

```python
import math

import jax
import jax.numpy as jnp
from jax import lax
from jax.experimental import pallas as pl
from jax.experimental.pallas import tpu as pltpu
from jax.sharding import PartitionSpec as P

D = 128
BLK = 256
NB = 16
CH = NB // 2
TQ = 2 * BLK
WIN = NB * BLK
SUB = 256
LONG = 1792
SCALE = 1.0 / (math.sqrt(144) * 50.0)
EXPO = 50.0 * math.log2(math.e)
F32 = jnp.float32
BF = jnp.bfloat16
MESH = pl.DeviceIdType.MESH


def to(peer):
    return {"seq": peer}


def wait_bytes(view, sem):
    pltpu.make_async_copy(view, view, sem).wait()


def cols(index):
    return pl.ds(pl.multiple_of(index * D, D), D)


def rows(index):
    return pl.ds(pl.multiple_of(index * BLK, BLK), BLK)


def pair(index):
    return pl.ds(pl.multiple_of(index * TQ, TQ), TQ)


def send(src, dst, send_sem, recv_sem, peer):
    pltpu.make_async_remote_copy(
        src_ref=src, dst_ref=dst, send_sem=send_sem, recv_sem=recv_sem,
        device_id=to(peer), device_id_type=MESH,
    ).start()


def attend(first, q, do, dl, live, ek, ev, g, p_s, h_s, wq, wd):
    wq[...] = q.T
    wd[...] = do.T

    def scores(r0, n):
        return jnp.dot(ek[pl.ds(r0, n), :], wq[...], preferred_element_type=F32) * SCALE

    def dprob(r0, n):
        return jnp.dot(ev[pl.ds(r0, n), :], wd[...], preferred_element_type=F32) - dl

    def weigh(at, x, dp):
        n = x.shape[0]
        th = jnp.tanh(x)
        p = jnp.exp2(EXPO * th)
        p_s[at, :] = p
        h_s[at, :] = p * (1.0 - th * th) * dp
        return p.reshape(n // 8, 8, TQ).sum(0)

    def older(n, start):
        row = lax.broadcasted_iota(jnp.int32, (n, TQ), 0) + start
        return row > lax.broadcasted_iota(jnp.int32, (n, TQ), 1)

    total = jnp.zeros((8, TQ), F32)
    for s in range(TQ // SUB):
        old = older(SUB, s * SUB)
        ra = pl.multiple_of(first + s * SUB, SUB)
        rb = pl.multiple_of(first + WIN + s * SUB, SUB)
        x = jnp.where(old, scores(ra, SUB), scores(rb, SUB))
        dp = jnp.where(old, dprob(ra, SUB), dprob(rb, SUB))
        total = total + weigh(pl.ds(s * SUB, SUB), x, dp)

    def forward(m, total):
        r0 = pl.multiple_of(first + TQ + m * LONG, BLK)
        at = pl.multiple_of(TQ + m * LONG, BLK)
        for s in range(LONG // SUB):
            total = total + weigh(
                pl.ds(at + s * SUB, SUB), scores(r0 + s * SUB, SUB), dprob(r0 + s * SUB, SUB)
            )
        return total

    total = lax.fori_loop(0, (WIN - TQ) // LONG, forward, total)
    inv = jnp.where(live, 1.0 / jnp.sum(total, axis=0, keepdims=True), 0.0)
    inv12 = inv * (1.0 / 12.0)

    def add(r0, n, p, h):
        p = p.astype(BF)
        h = h.astype(BF)
        g[1, pl.ds(r0, n), :] += jnp.dot(p, do, preferred_element_type=F32)
        g[0, pl.ds(r0, n), :] += jnp.dot(h, q, preferred_element_type=F32)
        return lax.dot_general(
            ek[pl.ds(r0, n), :], h, (((0,), (0,)), ((), ())), preferred_element_type=F32
        )

    old = older(TQ, 0)
    p = p_s[0:TQ, :] * inv
    h = h_s[0:TQ, :] * inv12
    zero = jnp.zeros_like(p)
    acc = add(first, TQ, jnp.where(old, p, zero), jnp.where(old, h, zero))
    acc = acc + add(first + WIN, TQ, jnp.where(old, zero, p), jnp.where(old, zero, h))

    def backward(m, acc):
        r0 = pl.multiple_of(first + TQ + m * LONG, BLK)
        at = pl.ds(pl.multiple_of(TQ + m * LONG, BLK), LONG)
        return acc + add(r0, LONG, p_s[at, :] * inv, h_s[at, :] * inv12)

    acc = lax.fori_loop(0, (WIN - TQ) // LONG, backward, acc)
    return acc.T.astype(BF)


def whole(
    bit_ref, q_ref, do_ref, dl_ref, k_ref, v_ref, tk_ref, tv_ref,
    gq_ref, gkv_ref,
    qd, dlg, tails, ek, ev, g, p_s, h_s, wq, wd, dqb, give, theirs, both,
    send_q, send_l, send_kv, send_rel, recv_q, recv_l, recv_kv, recv_rel, local,
    send_d, recv_d, send_x, recv_x, send_g, recv_g,
):
    me = lax.axis_index("seq")
    chip = me // 2
    core = lax.rem(me, 2)
    partner = chip * 2 + 1 - core
    bits = [bit_ref[b : b + 1, :] > 0 for b in range(4)]

    def kv_slots(device):
        return (
            (tk_ref, tails.at[0, rows(device)]),
            (k_ref, ek.at[rows(NB + device)]),
            (tv_ref, tails.at[1, rows(device)]),
            (v_ref, ev.at[rows(NB + device)]),
        )

    own = [
        pltpu.make_async_copy(src.at[:, cols(chip)], dst, local.at[a])
        for a, (src, dst) in enumerate(kv_slots(me))
    ]
    own.append(pltpu.make_async_copy(q_ref.at[:, cols(me)], qd.at[0, rows(me)], local.at[4]))
    own.append(pltpu.make_async_copy(do_ref.at[:, cols(me)], qd.at[1, rows(me)], local.at[5]))
    own.append(pltpu.make_async_copy(dl_ref.at[me], dlg.at[me], local.at[6]))
    for copy in own:
        copy.start()

    barrier = pltpu.get_barrier_semaphore()

    def greet(step, carry):
        pl.semaphore_signal(
            barrier, inc=1, device_id=to(lax.rem(me + step, NB)), device_id_type=MESH
        )
        return carry

    lax.fori_loop(1, NB, greet, 0)
    pl.semaphore_wait(barrier, NB - 1)

    def send_chip(step, carry):
        other = lax.rem(chip + step, CH)
        for a, (src, dst) in enumerate(kv_slots(me)):
            send(src.at[:, cols(other)], dst, send_kv.at[a, other], recv_kv.at[a, chip], other * 2 + core)
        return carry

    lax.fori_loop(1, CH, send_chip, 0)
    for a, (src, dst) in enumerate(kv_slots(me)):
        send(src.at[:, cols(chip)], dst, send_rel.at[a, chip], recv_rel.at[a, chip], partner)

    def send_peer(peer):
        send(q_ref.at[:, cols(peer)], qd.at[0, rows(me)], send_q.at[0, peer], recv_q.at[0, me], peer)
        send(do_ref.at[:, cols(peer)], qd.at[1, rows(me)], send_q.at[1, peer], recv_q.at[1, me], peer)
        send(dl_ref.at[peer], dlg.at[me], send_l.at[peer], recv_l.at[me], peer)

    send_peer(partner)

    def send_step(step, carry):
        other = lax.rem(chip + CH - step, CH)
        send_peer(other * 2)
        send_peer(other * 2 + 1)
        return carry

    lax.fori_loop(1, CH, send_step, 0)
    g[...] = jnp.zeros_like(g)

    def relay(step, carry):
        other = lax.rem(chip + CH - step, CH)
        for a, (src, view) in enumerate(kv_slots(other * 2 + core)):
            wait_bytes(view, recv_kv.at[a, other])
            send(view, view, send_rel.at[a, other], recv_rel.at[a, other], partner)
        return carry

    lax.fori_loop(1, CH, relay, 0)

    def arrived(step, carry):
        other = lax.rem(chip + step, CH)
        for a, (src, view) in enumerate(kv_slots(other * 2 + 1 - core)):
            wait_bytes(view, recv_rel.at[a, other])
        return carry

    lax.fori_loop(0, CH, arrived, 0)
    for copy in own:
        copy.wait()

    def sent(step, carry):
        other = lax.rem(chip + step, CH)
        for a, (src, view) in enumerate(kv_slots(other * 2 + core)):
            wait_bytes(view, send_rel.at[a, other])
        return carry

    lax.fori_loop(0, CH, sent, 0)

    def pick(read, low, high, shift):
        def block(j):
            a = [read(lax.rem(j + NB + k * shift, NB)).astype(F32) for k in range(4)]
            even = jnp.where(bits[low], a[1], a[0])
            odd = jnp.where(bits[low], a[3], a[2])
            return jnp.where(bits[high], odd, even).astype(BF)

        return block

    def near(a):
        return pick(lambda j: tails[a, rows(j), :], 0, 1, 1)

    def far(a):
        return pick(lambda j: give[a, rows(j), :], 2, 3, 4)

    def turn_near(j, carry):
        give[0, rows(j), :] = near(0)(j)
        give[1, rows(j), :] = near(1)(j)
        return carry

    def turn_far(j, carry):
        ek[rows(j), :] = far(0)(j)
        ev[rows(j), :] = far(1)(j)
        return carry

    lax.fori_loop(0, NB, turn_near, 0)
    lax.fori_loop(0, NB, turn_far, 0)

    def send_dq(tile):
        for peer in (tile * 2, tile * 2 + 1):

            @pl.when(peer != me)
            def _():
                send(dqb.at[rows(peer)], gq_ref.at[:, cols(me)], send_d.at[peer], recv_d.at[me], peer)

    def step_tile(step, carry):
        tile = lax.rem(chip + step, CH)
        for peer in (tile * 2, tile * 2 + 1):

            @pl.when(peer != me)
            def _():
                wait_bytes(qd.at[0, rows(peer)], recv_q.at[0, peer])
                wait_bytes(qd.at[1, rows(peer)], recv_q.at[1, peer])
                wait_bytes(dlg.at[peer], recv_l.at[peer])

        @pl.when(step > 0)
        def _():
            send_dq(lax.rem(chip + step + CH - 1, CH))

        first = pl.multiple_of(tile * TQ, TQ)
        low = dlg[tile * 2]
        high = dlg[tile * 2 + 1]
        dl = jnp.concatenate([low[:, :BLK], high[:, :BLK]], axis=1)
        lane = lax.broadcasted_iota(jnp.int32, (1, D), 1).astype(F32)
        live = jnp.concatenate(
            [
                lane < low[:, BLK:],
                lane + D < low[:, BLK:],
                lane < high[:, BLK:],
                lane + D < high[:, BLK:],
            ],
            axis=1,
        )
        dqb[pair(tile), :] = attend(
            first, qd[0, pair(tile), :], qd[1, pair(tile), :], dl, live,
            ek, ev, g, p_s, h_s, wq, wd,
        )
        return carry

    lax.fori_loop(0, CH, step_tile, 0)

    def tile_at(step):
        return lax.rem(chip + 1 + step, CH)

    def stretch(tile):
        return pl.ds(pl.multiple_of(WIN + tile * TQ, TQ), TQ)

    def prepare(tile):
        give[1, pair(tile), :] = g[1 - core, stretch(tile), :].astype(BF)

    def exchange(tile):
        send(give.at[1, pair(tile)], theirs.at[1, pair(tile)], send_x.at[tile], recv_x.at[tile], partner)

    prepare(tile_at(0))
    send_dq(lax.rem(chip + CH - 1, CH))

    def give_step(step, carry):
        prepare(tile_at(step))
        exchange(tile_at(step - 1))
        return carry

    lax.fori_loop(1, CH, give_step, 0)
    mine = pltpu.make_async_copy(dqb.at[rows(me)], gq_ref.at[:, cols(me)], local.at[0])
    mine.start()
    give[0] = g[1 - core, 0:WIN, :].astype(BF)
    exchange(tile_at(CH - 1))

    def combine(tile):
        wait_bytes(theirs.at[1, pair(tile)], recv_x.at[tile])
        both[1, pair(tile), :] = (
            g[core, stretch(tile), :] + theirs[1, pair(tile), :].astype(F32)
        ).astype(BF)

    def ship(buffer, kind, tile):
        for peer in (tile * 2, tile * 2 + 1):

            @pl.when(peer != me)
            def _():
                send(
                    buffer.at[1, rows(peer)], gkv_ref.at[core, kind, :, cols(chip)],
                    send_g.at[kind, peer], recv_g.at[kind, me], peer,
                )

    combine(tile_at(0))
    send(give.at[0], theirs.at[0], send_x.at[CH], recv_x.at[CH], partner)

    def ship_step(step, carry):
        combine(tile_at(step))
        ship(both, 1, tile_at(step - 1))
        return carry

    lax.fori_loop(1, CH, ship_step, 0)
    last = pltpu.make_async_copy(both.at[1, rows(me)], gkv_ref.at[core, 1, :, cols(chip)], local.at[1])
    last.start()
    ship(both, 1, chip)
    wait_bytes(theirs.at[0], recv_x.at[CH])
    both[0] = (g[core, 0:WIN, :] + theirs[0].astype(F32)).astype(BF)

    def back_near(j, carry):
        tails[0, rows(j), :] = pick(lambda i: both[0, rows(i), :], 0, 1, -1)(j)
        return carry

    def back_far(j, carry):
        tails[1, rows(j), :] = pick(lambda i: tails[0, rows(i), :], 2, 3, -4)(j)
        return carry

    lax.fori_loop(0, NB, back_near, 0)
    lax.fori_loop(0, NB, back_far, 0)
    tail = pltpu.make_async_copy(tails.at[1, rows(me)], gkv_ref.at[core, 0, :, cols(chip)], local.at[2])
    tail.start()

    def ship_tail(step, carry):
        ship(tails, 0, tile_at(step))
        return carry

    lax.fori_loop(0, CH, ship_tail, 0)

    def finish(step, carry):
        peer = lax.rem(me + step, NB)
        wait_bytes(qd.at[0, rows(peer)], send_q.at[0, peer])
        wait_bytes(qd.at[1, rows(peer)], send_q.at[1, peer])
        wait_bytes(dlg.at[peer], send_l.at[peer])
        wait_bytes(dqb.at[rows(peer)], send_d.at[peer])
        wait_bytes(dqb.at[rows(peer)], recv_d.at[peer])
        for kind in range(2):
            wait_bytes(tails.at[1, rows(peer)], send_g.at[kind, peer])
            wait_bytes(tails.at[1, rows(peer)], recv_g.at[kind, peer])
        return carry

    lax.fori_loop(1, NB, finish, 0)

    def finish_chip(step, carry):
        other = lax.rem(chip + step, CH)
        for a, (src, view) in enumerate(kv_slots(other * 2 + core)):
            wait_bytes(view, send_kv.at[a, other])
        return carry

    lax.fori_loop(1, CH, finish_chip, 0)

    def finish_x(tile, carry):
        wait_bytes(theirs.at[1, pair(tile)], send_x.at[tile])
        return carry

    lax.fori_loop(0, CH, finish_x, 0)
    wait_bytes(theirs.at[0], send_x.at[CH])
    mine.wait()
    last.wait()
    tail.wait()


def run(bits, q, do, dl, k, v, tk, tv):
    any_ = pl.BlockSpec(memory_space=pl.ANY)
    dma = pltpu.SemaphoreType.DMA
    vm = pltpu.VMEM
    return pl.pallas_call(
        whole,
        in_specs=[pl.BlockSpec(memory_space=pltpu.VMEM)] + [any_] * 7,
        out_specs=[any_] * 2,
        out_shape=[
            jax.ShapeDtypeStruct((BLK, NB * D), BF),
            jax.ShapeDtypeStruct((2, 2, BLK, CH * D), BF),
        ],
        scratch_shapes=[
            vm((2, WIN, D), BF), vm(dl.shape, F32), vm((2, WIN, D), BF),
            vm((2 * WIN, D), BF), vm((2 * WIN, D), BF), vm((2, 2 * WIN, D), F32),
            vm((WIN, TQ), F32), vm((WIN, TQ), F32), vm((D, TQ), BF), vm((D, TQ), BF),
            vm((WIN, D), BF), vm((2, WIN, D), BF), vm((2, WIN, D), BF), vm((2, WIN, D), BF),
            dma((2, NB)), dma((NB,)), dma((4, CH)), dma((4, CH)),
            dma((2, NB)), dma((NB,)), dma((4, CH)), dma((4, CH)), dma((7,)),
            dma((NB,)), dma((NB,)), dma((CH + 1,)), dma((CH + 1,)), dma((2, NB)), dma((2, NB)),
        ],
        compiler_params=pltpu.CompilerParams(
            collective_id=0, has_side_effects=True, vmem_limit_bytes=62 << 20
        ),
    )(bits, q, do, dl, k, v, tk, tv)


def per_device(query, keys, values, tail_keys, cached_tail_values, output_gradient, forward_output, stretch_index, valid_counts):
    delta = jnp.sum(
        (output_gradient.astype(F32) * forward_output.astype(F32)).reshape(BLK, NB, D), axis=2
    )
    count = jnp.full((NB, D), valid_counts[0].astype(F32))
    extra = jnp.concatenate([delta.T, count], axis=1)[:, None, :]
    powers = jnp.left_shift(1, jnp.arange(8, dtype=jnp.int32))
    bits = jnp.broadcast_to(jnp.bitwise_and(stretch_index, powers)[:, None], (8, D))
    gq, gkv = run(
        bits, query, output_gradient, extra, keys, values, tail_keys, cached_tail_values
    )
    return gq, gkv[0, 1], gkv[1, 1], gkv[0, 0], gkv[1, 0]


def solution(mesh):
    tokens = P(("section", "seq"), None)
    return jax.shard_map(
        per_device,
        mesh=mesh,
        in_specs=(tokens,) * 7 + (P(), P(("section", "seq"))),
        out_specs=(tokens,) * 5,
        check_vma=False,
    )
```

```python
import math

import jax
import jax.numpy as jnp
from jax import lax
from jax.experimental import pallas as pl
from jax.experimental.pallas import tpu as pltpu
from jax.sharding import PartitionSpec as P

D = 128
BLK = 256
NB = 16
CH = NB // 2
TQ = 2 * BLK
WIN = NB * BLK
SUB = 256
LONG = 1792
SCALE = 1.0 / (math.sqrt(144) * 50.0)
EXPO = 50.0 * math.log2(math.e)
F32 = jnp.float32
BF = jnp.bfloat16
MESH = pl.DeviceIdType.MESH


def to(peer):
    return {"seq": peer}


def wait_bytes(view, sem):
    pltpu.make_async_copy(view, view, sem).wait()


def cols(index):
    return pl.ds(pl.multiple_of(index * D, D), D)


def rows(index):
    return pl.ds(pl.multiple_of(index * BLK, BLK), BLK)


def pair(index):
    return pl.ds(pl.multiple_of(index * TQ, TQ), TQ)


def send(src, dst, send_sem, recv_sem, peer):
    pltpu.make_async_remote_copy(
        src_ref=src, dst_ref=dst, send_sem=send_sem, recv_sem=recv_sem,
        device_id=to(peer), device_id_type=MESH,
    ).start()


def attend(first, q, do, dl, live, ek, ev, g, p_s, u_s, d_s, wq, wd):
    wq[...] = q.T
    wd[...] = do.T

    def scores(r0, n):
        return jnp.dot(ek[pl.ds(r0, n), :], wq[...], preferred_element_type=F32) * SCALE

    def dprob(r0, n):
        return jnp.dot(ev[pl.ds(r0, n), :], wd[...], preferred_element_type=F32)

    def weigh(at, x, dp):
        n = x.shape[0]
        th = jnp.tanh(x)
        p = jnp.exp2(EXPO * th)
        p_s[at, :] = p
        u_s[at, :] = 1.0 - th * th
        d_s[at, :] = dp
        return p.reshape(n // 8, 8, TQ).sum(0)

    def older(n, start):
        row = lax.broadcasted_iota(jnp.int32, (n, TQ), 0) + start
        return row > lax.broadcasted_iota(jnp.int32, (n, TQ), 1)

    total = jnp.zeros((8, TQ), F32)
    for s in range(TQ // SUB):
        old = older(SUB, s * SUB)
        ra = pl.multiple_of(first + s * SUB, SUB)
        rb = pl.multiple_of(first + WIN + s * SUB, SUB)
        x = jnp.where(old, scores(ra, SUB), scores(rb, SUB))
        dp = jnp.where(old, dprob(ra, SUB), dprob(rb, SUB))
        total = total + weigh(pl.ds(s * SUB, SUB), x, dp)

    def forward(m, total):
        r0 = pl.multiple_of(first + TQ + m * LONG, BLK)
        at = pl.multiple_of(TQ + m * LONG, BLK)
        for s in range(LONG // SUB):
            total = total + weigh(
                pl.ds(at + s * SUB, SUB), scores(r0 + s * SUB, SUB), dprob(r0 + s * SUB, SUB)
            )
        return total

    total = lax.fori_loop(0, (WIN - TQ) // LONG, forward, total)
    inv = jnp.where(live, 1.0 / jnp.sum(total, axis=0, keepdims=True), 0.0)

    def weights(at):
        p = p_s[at, :] * inv
        return p, (p * u_s[at, :]) * ((d_s[at, :] - dl) * (1.0 / 12.0))

    def add(r0, n, p, h):
        p = p.astype(BF)
        h = h.astype(BF)
        g[1, pl.ds(r0, n), :] += jnp.dot(p, do, preferred_element_type=F32)
        g[0, pl.ds(r0, n), :] += jnp.dot(h, q, preferred_element_type=F32)
        return lax.dot_general(
            ek[pl.ds(r0, n), :], h, (((0,), (0,)), ((), ())), preferred_element_type=F32
        )

    old = older(TQ, 0)
    p, h = weights(pl.ds(0, TQ))
    zero = jnp.zeros_like(p)
    acc = add(first, TQ, jnp.where(old, p, zero), jnp.where(old, h, zero))
    acc = acc + add(first + WIN, TQ, jnp.where(old, zero, p), jnp.where(old, zero, h))

    def backward(m, acc):
        r0 = pl.multiple_of(first + TQ + m * LONG, BLK)
        at = pl.ds(pl.multiple_of(TQ + m * LONG, BLK), LONG)
        return acc + add(r0, LONG, *weights(at))

    acc = lax.fori_loop(0, (WIN - TQ) // LONG, backward, acc)
    return acc.T.astype(BF)


def whole(
    bit_ref, q_ref, do_ref, fo_ref, k_ref, v_ref, tk_ref, tv_ref,
    gq_ref, gkv_ref,
    qd, dlg, dls, tails, ek, ev, g, p_s, u_s, d_s, wq, wd, give, theirs,
    send_q, send_l, send_kv, send_rel, recv_q, recv_l, recv_kv, recv_rel, local,
    send_s, recv_s, send_d, recv_d, send_x, recv_x, send_g, recv_g,
):
    me = lax.axis_index("seq")
    chip = me // 2
    core = lax.rem(me, 2)
    partner = chip * 2 + 1 - core
    dqb = tails.at[0]
    both = qd
    bits = [bit_ref[b : b + 1, :] > 0 for b in range(4)]

    def kv_slots(device):
        return (
            (tk_ref, tails.at[0, rows(device)]),
            (k_ref, ek.at[rows(NB + device)]),
            (tv_ref, tails.at[1, rows(device)]),
            (v_ref, ev.at[rows(NB + device)]),
        )

    own = [
        pltpu.make_async_copy(src.at[:, cols(chip)], dst, local.at[a])
        for a, (src, dst) in enumerate(kv_slots(me))
    ]
    own.append(pltpu.make_async_copy(q_ref.at[:, cols(me)], qd.at[0, rows(me)], local.at[4]))
    own.append(pltpu.make_async_copy(do_ref.at[:, cols(me)], qd.at[1, rows(me)], local.at[5]))

    def fetch(h, carry):
        for a, src in enumerate((do_ref, fo_ref)):
            pltpu.make_async_copy(src.at[:, cols(h)], give.at[a, rows(h)], local.at[6 + a]).start()
        return carry

    lax.fori_loop(0, NB, fetch, 0)
    for copy in own:
        copy.start()

    barrier = pltpu.get_barrier_semaphore()

    def greet(step, carry):
        pl.semaphore_signal(
            barrier, inc=1, device_id=to(lax.rem(me + step, NB)), device_id_type=MESH
        )
        return carry

    lax.fori_loop(1, NB, greet, 0)
    pl.semaphore_wait(barrier, NB - 1)

    def send_chip(other, kinds):
        slots = kv_slots(me)
        for a in kinds:
            src, dst = slots[a]
            send(src.at[:, cols(other)], dst, send_kv.at[a, other], recv_kv.at[a, chip], other * 2 + core)

    def send_tail(step, carry):
        send_chip(lax.rem(chip + step, CH), (0, 2))
        return carry

    def send_later(other, carry):
        send_chip(other, (1, 3))
        return carry

    lax.fori_loop(1, CH, send_tail, 0)
    lax.fori_loop(chip + 1, CH, send_later, 0)
    for a, (src, dst) in enumerate(kv_slots(me)):
        send(src.at[:, cols(chip)], dst, send_rel.at[a, chip], recv_rel.at[a, chip], partner)

    def send_peer(peer):
        send(q_ref.at[:, cols(peer)], qd.at[0, rows(me)], send_q.at[0, peer], recv_q.at[0, me], peer)
        send(do_ref.at[:, cols(peer)], qd.at[1, rows(me)], send_q.at[1, peer], recv_q.at[1, me], peer)

    send_peer(partner)

    def send_step(step, carry):
        other = lax.rem(chip + CH - step, CH)
        for peer in (other * 2, other * 2 + 1):

            @pl.when(other < chip)
            def _():
                for a, src, dst in ((0, k_ref, ek), (1, v_ref, ev)):
                    send(src.at[:, cols(other)], dst.at[rows(NB + me)], send_s.at[a, peer], recv_s.at[a, me], peer)

            send_peer(peer)
        return carry

    lax.fori_loop(1, CH, send_step, 0)
    for a in range(2):
        wait_bytes(give.at[a], local.at[6 + a])
    for h in range(NB):
        at = slice(h * BLK, (h + 1) * BLK)
        product = give[0, at, :].astype(F32) * give[1, at, :].astype(F32)
        dls[h, :, 0:BLK] = jnp.sum(product.T, axis=0, keepdims=True)
        dls[h, :, BLK:] = bit_ref[4:5, :].astype(F32)

    g[...] = jnp.zeros_like(g)
    dlg[me] = dls[me]

    def send_delta(step, carry):
        peer = lax.rem(me + NB - step, NB)
        send(dls.at[peer], dlg.at[me], send_l.at[peer], recv_l.at[me], peer)
        return carry

    lax.fori_loop(1, NB, send_delta, 0)

    def relay(other, kinds):
        slots = kv_slots(other * 2 + core)
        for a in kinds:
            view = slots[a][1]
            wait_bytes(view, recv_kv.at[a, other])
            send(view, view, send_rel.at[a, other], recv_rel.at[a, other], partner)

    def relay_tail(step, carry):
        relay(lax.rem(chip + CH - step, CH), (0, 2))
        return carry

    def relay_early(step, carry):
        relay(chip - step, (1, 3))
        return carry

    lax.fori_loop(1, CH, relay_tail, 0)
    lax.fori_loop(1, chip + 1, relay_early, 0)

    def arrived(other, kinds):
        slots = kv_slots(other * 2 + 1 - core)
        for a in kinds:
            wait_bytes(slots[a][1], recv_rel.at[a, other])
            wait_bytes(slots[a][1], send_rel.at[a, other])

    def arrived_tail(other, carry):
        arrived(other, (0, 2))
        return carry

    def arrived_early(other, carry):
        arrived(other, (1, 3))
        return carry

    lax.fori_loop(0, CH, arrived_tail, 0)
    lax.fori_loop(0, chip + 1, arrived_early, 0)
    for copy in own:
        copy.wait()

    def pick(read, low, high, shift):
        def block(j):
            a = [read(lax.rem(j + NB + k * shift, NB)).astype(F32) for k in range(4)]
            even = jnp.where(bits[low], a[1], a[0])
            odd = jnp.where(bits[low], a[3], a[2])
            return jnp.where(bits[high], odd, even).astype(BF)

        return block

    def near(a):
        return pick(lambda j: tails[a, rows(j), :], 0, 1, 1)

    def far(a):
        return pick(lambda j: give[a, rows(j), :], 2, 3, 4)

    def turn_near(j, carry):
        give[0, rows(j), :] = near(0)(j)
        give[1, rows(j), :] = near(1)(j)
        return carry

    def turn_far(j, carry):
        ek[rows(j), :] = far(0)(j)
        ev[rows(j), :] = far(1)(j)
        return carry

    lax.fori_loop(0, NB, turn_near, 0)
    lax.fori_loop(0, NB, turn_far, 0)

    def send_dq(tile):
        for peer in (tile * 2, tile * 2 + 1):

            @pl.when(peer != me)
            def _():
                send(dqb.at[rows(peer)], gq_ref.at[:, cols(me)], send_d.at[peer], recv_d.at[me], peer)

    def step_tile(step, carry):
        tile = lax.rem(chip + step, CH)
        for peer in (tile * 2, tile * 2 + 1):

            @pl.when(peer != me)
            def _():
                wait_bytes(qd.at[0, rows(peer)], recv_q.at[0, peer])
                wait_bytes(qd.at[1, rows(peer)], recv_q.at[1, peer])
                wait_bytes(dlg.at[peer], recv_l.at[peer])

            @pl.when(tile > chip)
            def _():
                wait_bytes(ek.at[rows(NB + peer)], recv_s.at[0, peer])
                wait_bytes(ev.at[rows(NB + peer)], recv_s.at[1, peer])

        @pl.when(step > 0)
        def _():
            send_dq(lax.rem(chip + step + CH - 1, CH))

        first = pl.multiple_of(tile * TQ, TQ)
        low = dlg[tile * 2]
        high = dlg[tile * 2 + 1]
        dl = jnp.concatenate([low[:, :BLK], high[:, :BLK]], axis=1)
        lane = lax.broadcasted_iota(jnp.int32, (1, D), 1).astype(F32)
        live = jnp.concatenate(
            [
                lane < low[:, BLK:],
                lane + D < low[:, BLK:],
                lane < high[:, BLK:],
                lane + D < high[:, BLK:],
            ],
            axis=1,
        )
        dqb[pair(tile), :] = attend(
            first, qd[0, pair(tile), :], qd[1, pair(tile), :], dl, live,
            ek, ev, g, p_s, u_s, d_s, wq, wd,
        )
        return carry

    lax.fori_loop(0, CH, step_tile, 0)

    def tile_at(step):
        return lax.rem(chip + 1 + step, CH)

    def stretch(tile):
        return pl.ds(pl.multiple_of(WIN + tile * TQ, TQ), TQ)

    def prepare(tile):
        give[1, pair(tile), :] = g[1 - core, stretch(tile), :].astype(BF)

    def exchange(tile):
        send(give.at[1, pair(tile)], theirs.at[1, pair(tile)], send_x.at[tile], recv_x.at[tile], partner)

    prepare(tile_at(0))
    send_dq(lax.rem(chip + CH - 1, CH))

    def give_step(step, carry):
        prepare(tile_at(step))
        exchange(tile_at(step - 1))
        return carry

    lax.fori_loop(1, CH, give_step, 0)
    mine = pltpu.make_async_copy(dqb.at[rows(me)], gq_ref.at[:, cols(me)], local.at[0])
    mine.start()
    give[0] = g[1 - core, 0:WIN, :].astype(BF)
    exchange(tile_at(CH - 1))

    def combine(tile):
        wait_bytes(theirs.at[1, pair(tile)], recv_x.at[tile])
        both[1, pair(tile), :] = (
            g[core, stretch(tile), :] + theirs[1, pair(tile), :].astype(F32)
        ).astype(BF)

    def ship(buffer, kind, tile):
        for peer in (tile * 2, tile * 2 + 1):

            @pl.when(peer != me)
            def _():
                send(
                    buffer.at[1, rows(peer)], gkv_ref.at[core, kind, :, cols(chip)],
                    send_g.at[kind, peer], recv_g.at[kind, me], peer,
                )

    combine(tile_at(0))
    send(give.at[0], theirs.at[0], send_x.at[CH], recv_x.at[CH], partner)

    def ship_step(step, carry):
        combine(tile_at(step))
        ship(both, 1, tile_at(step - 1))
        return carry

    lax.fori_loop(1, CH, ship_step, 0)
    last = pltpu.make_async_copy(both.at[1, rows(me)], gkv_ref.at[core, 1, :, cols(chip)], local.at[1])
    last.start()
    ship(both, 1, chip)
    wait_bytes(theirs.at[0], recv_x.at[CH])
    mine.wait()

    def free_dq(step, carry):
        peer = lax.rem(me + step, NB)
        wait_bytes(dqb.at[rows(peer)], send_d.at[peer])
        return carry

    lax.fori_loop(1, NB, free_dq, 0)
    both[0] = (g[core, 0:WIN, :] + theirs[0].astype(F32)).astype(BF)

    def back_near(j, carry):
        tails[0, rows(j), :] = pick(lambda i: both[0, rows(i), :], 0, 1, -1)(j)
        return carry

    def back_far(j, carry):
        tails[1, rows(j), :] = pick(lambda i: tails[0, rows(i), :], 2, 3, -4)(j)
        return carry

    lax.fori_loop(0, NB, back_near, 0)
    lax.fori_loop(0, NB, back_far, 0)
    tail = pltpu.make_async_copy(tails.at[1, rows(me)], gkv_ref.at[core, 0, :, cols(chip)], local.at[2])
    tail.start()

    def ship_tail(step, carry):
        ship(tails, 0, tile_at(step))
        return carry

    lax.fori_loop(0, CH, ship_tail, 0)

    def finish(step, carry):
        peer = lax.rem(me + step, NB)
        wait_bytes(qd.at[0, rows(peer)], send_q.at[0, peer])
        wait_bytes(qd.at[1, rows(peer)], send_q.at[1, peer])
        wait_bytes(dlg.at[peer], send_l.at[peer])
        wait_bytes(dqb.at[rows(peer)], recv_d.at[peer])
        for kind in range(2):
            wait_bytes(tails.at[1, rows(peer)], send_g.at[kind, peer])
            wait_bytes(tails.at[1, rows(peer)], recv_g.at[kind, peer])
        return carry

    lax.fori_loop(1, NB, finish, 0)

    def finish_tail(step, carry):
        other = lax.rem(chip + step, CH)
        for a in (0, 2):
            wait_bytes(dqb.at[rows(other)], send_kv.at[a, other])
        return carry

    def finish_later(other, carry):
        for a in (1, 3):
            wait_bytes(dqb.at[rows(other)], send_kv.at[a, other])
        return carry

    def finish_early(peer, carry):
        for a in range(2):
            wait_bytes(dqb.at[rows(peer)], send_s.at[a, peer])
        return carry

    lax.fori_loop(1, CH, finish_tail, 0)
    lax.fori_loop(chip + 1, CH, finish_later, 0)
    lax.fori_loop(0, chip * 2, finish_early, 0)

    def finish_x(tile, carry):
        wait_bytes(theirs.at[1, pair(tile)], send_x.at[tile])
        return carry

    lax.fori_loop(0, CH, finish_x, 0)
    wait_bytes(theirs.at[0], send_x.at[CH])
    last.wait()
    tail.wait()


def run(bits, q, do, fo, k, v, tk, tv):
    any_ = pl.BlockSpec(memory_space=pl.ANY)
    dma = pltpu.SemaphoreType.DMA
    vm = pltpu.VMEM
    return pl.pallas_call(
        whole,
        in_specs=[pl.BlockSpec(memory_space=pltpu.VMEM)] + [any_] * 7,
        out_specs=[any_] * 2,
        out_shape=[
            jax.ShapeDtypeStruct((BLK, NB * D), BF),
            jax.ShapeDtypeStruct((2, 2, BLK, CH * D), BF),
        ],
        scratch_shapes=[
            vm((2, WIN, D), BF), vm((NB, 1, BLK + D), F32), vm((NB, 1, BLK + D), F32),
            vm((2, WIN, D), BF),
            vm((2 * WIN, D), BF), vm((2 * WIN, D), BF), vm((2, 2 * WIN, D), F32),
            vm((WIN, TQ), F32), vm((WIN, TQ), F32), vm((WIN, TQ), F32), vm((D, TQ), BF), vm((D, TQ), BF),
            vm((2, WIN, D), BF), vm((2, WIN, D), BF),
            dma((2, NB)), dma((NB,)), dma((4, CH)), dma((4, CH)),
            dma((2, NB)), dma((NB,)), dma((4, CH)), dma((4, CH)), dma((8,)),
            dma((2, NB)), dma((2, NB)), dma((NB,)), dma((NB,)), dma((CH + 1,)), dma((CH + 1,)), dma((2, NB)), dma((2, NB)),
        ],
        compiler_params=pltpu.CompilerParams(
            collective_id=0, has_side_effects=True, vmem_limit_bytes=62 << 20
        ),
    )(bits, q, do, fo, k, v, tk, tv)


def per_device(query, keys, values, tail_keys, cached_tail_values, output_gradient, forward_output, stretch_index, valid_counts):
    powers = jnp.left_shift(1, jnp.arange(8, dtype=jnp.int32))
    rank = jnp.arange(8, dtype=jnp.int32)
    table = jnp.where(rank < 4, jnp.bitwise_and(stretch_index, powers), valid_counts)
    bits = jnp.broadcast_to(table[:, None], (8, D))
    gq, gkv = run(
        bits, query, output_gradient, forward_output, keys, values, tail_keys, cached_tail_values
    )
    return gq, gkv[0, 1], gkv[1, 1], gkv[0, 0], gkv[1, 0]


def solution(mesh):
    tokens = P(("section", "seq"), None)
    return jax.shard_map(
        per_device,
        mesh=mesh,
        in_specs=(tokens,) * 7 + (P(), P(("section", "seq"))),
        out_specs=(tokens,) * 5,
        check_vma=False,
    )
```

```python
import math

import jax
import jax.numpy as jnp
from jax import lax
from jax.experimental import pallas as pl
from jax.experimental.pallas import tpu as pltpu
from jax.sharding import PartitionSpec as P

D = 128
BLK = 256
NB = 16
CH = NB // 2
TQ = 2 * BLK
WIN = NB * BLK
SUB = 256
LONG = 1792
SCALE = 1.0 / (math.sqrt(144) * 50.0)
EXPO = 50.0 * math.log2(math.e)
F32 = jnp.float32
BF = jnp.bfloat16
MESH = pl.DeviceIdType.MESH


def to(peer):
    return {"seq": peer}


def wait_bytes(view, sem):
    pltpu.make_async_copy(view, view, sem).wait()


def cols(index):
    return pl.ds(pl.multiple_of(index * D, D), D)


def rows(index):
    return pl.ds(pl.multiple_of(index * BLK, BLK), BLK)


def pair(index):
    return pl.ds(pl.multiple_of(index * TQ, TQ), TQ)


def send(src, dst, send_sem, recv_sem, peer):
    pltpu.make_async_remote_copy(
        src_ref=src, dst_ref=dst, send_sem=send_sem, recv_sem=recv_sem,
        device_id=to(peer), device_id_type=MESH,
    ).start()


def attend(first, q, do, dl, live, ek, ev, g, p_s, u_s, d_s, wq, wd):
    wq[...] = q.T
    wd[...] = do.T

    def scores(r0, n):
        return jnp.dot(ek[pl.ds(r0, n), :], wq[...], preferred_element_type=F32) * SCALE

    def dprob(r0, n):
        return jnp.dot(ev[pl.ds(r0, n), :], wd[...], preferred_element_type=F32)

    def weigh(at, x, dp):
        n = x.shape[0]
        th = jnp.tanh(x)
        p = jnp.exp2(EXPO * th)
        p_s[at, :] = p
        u_s[at, :] = 1.0 - th * th
        d_s[at, :] = dp
        return p.reshape(n // 8, 8, TQ).sum(0)

    def older(n, start):
        row = lax.broadcasted_iota(jnp.int32, (n, TQ), 0) + start
        return row > lax.broadcasted_iota(jnp.int32, (n, TQ), 1)

    total = jnp.zeros((8, TQ), F32)
    for s in range(TQ // SUB):
        old = older(SUB, s * SUB)
        ra = pl.multiple_of(first + s * SUB, SUB)
        rb = pl.multiple_of(first + WIN + s * SUB, SUB)
        x = jnp.where(old, scores(ra, SUB), scores(rb, SUB))
        dp = jnp.where(old, dprob(ra, SUB), dprob(rb, SUB))
        total = total + weigh(pl.ds(s * SUB, SUB), x, dp)

    def forward(m, total):
        r0 = pl.multiple_of(first + TQ + m * LONG, BLK)
        at = pl.multiple_of(TQ + m * LONG, BLK)
        for s in range(LONG // SUB):
            total = total + weigh(
                pl.ds(at + s * SUB, SUB), scores(r0 + s * SUB, SUB), dprob(r0 + s * SUB, SUB)
            )
        return total

    total = lax.fori_loop(0, (WIN - TQ) // LONG, forward, total)
    inv = jnp.where(live, 1.0 / jnp.sum(total, axis=0, keepdims=True), 0.0)

    def weights(at):
        p = p_s[at, :] * inv
        return p, (p * u_s[at, :]) * ((d_s[at, :] - dl) * (1.0 / 12.0))

    def add(r0, n, p, h):
        p = p.astype(BF)
        h = h.astype(BF)
        g[1, pl.ds(r0, n), :] += jnp.dot(p, do, preferred_element_type=F32)
        g[0, pl.ds(r0, n), :] += jnp.dot(h, q, preferred_element_type=F32)
        return lax.dot_general(
            ek[pl.ds(r0, n), :], h, (((0,), (0,)), ((), ())), preferred_element_type=F32
        )

    old = older(TQ, 0)
    p, h = weights(pl.ds(0, TQ))
    zero = jnp.zeros_like(p)
    acc = add(first, TQ, jnp.where(old, p, zero), jnp.where(old, h, zero))
    acc = acc + add(first + WIN, TQ, jnp.where(old, zero, p), jnp.where(old, zero, h))

    def backward(m, acc):
        r0 = pl.multiple_of(first + TQ + m * LONG, BLK)
        at = pl.ds(pl.multiple_of(TQ + m * LONG, BLK), LONG)
        return acc + add(r0, LONG, *weights(at))

    acc = lax.fori_loop(0, (WIN - TQ) // LONG, backward, acc)
    return acc.T.astype(BF)


def whole(
    bit_ref, q_ref, do_ref, fo_ref, k_ref, v_ref, tk_ref, tv_ref,
    gq_ref, gkv_ref,
    qd, dlg, dls, tails, ek, ev, g, p_s, u_s, d_s, wq, wd, give, theirs,
    send_q, send_l, send_kv, send_rel, recv_q, recv_l, recv_kv, recv_rel, local,
    send_s, recv_s, send_d, recv_d, send_x, recv_x, send_g, recv_g,
):
    me = lax.axis_index("seq")
    chip = me // 2
    core = lax.rem(me, 2)
    partner = chip * 2 + 1 - core
    dqb = tails.at[0]
    both = qd
    bits = [bit_ref[b : b + 1, :] > 0 for b in range(4)]

    def kv_slots(device):
        return (
            (tk_ref, tails.at[0, rows(device)]),
            (k_ref, ek.at[rows(NB + device)]),
            (tv_ref, tails.at[1, rows(device)]),
            (v_ref, ev.at[rows(NB + device)]),
        )

    own = [
        pltpu.make_async_copy(src.at[:, cols(chip)], dst, local.at[a])
        for a, (src, dst) in enumerate(kv_slots(me))
    ]
    own.append(pltpu.make_async_copy(q_ref.at[:, cols(me)], qd.at[0, rows(me)], local.at[4]))
    own.append(pltpu.make_async_copy(do_ref.at[:, cols(me)], qd.at[1, rows(me)], local.at[5]))

    def fetch(h, carry):
        for a, src in enumerate((do_ref, fo_ref)):
            pltpu.make_async_copy(src.at[:, cols(h)], give.at[a, rows(h)], local.at[6 + a]).start()
        return carry

    lax.fori_loop(0, NB, fetch, 0)
    for copy in own:
        copy.start()

    barrier = pltpu.get_barrier_semaphore()

    def greet(step, carry):
        pl.semaphore_signal(
            barrier, inc=1, device_id=to(lax.rem(me + step, NB)), device_id_type=MESH
        )
        return carry

    lax.fori_loop(1, NB, greet, 0)
    pl.semaphore_wait(barrier, NB - 1)

    def send_chip(other, kinds):
        slots = kv_slots(me)
        for a in kinds:
            src, dst = slots[a]
            send(src.at[:, cols(other)], dst, send_kv.at[a, other], recv_kv.at[a, chip], other * 2 + core)

    def send_tail(step, carry):
        send_chip(lax.rem(chip + step, CH), (0, 2))
        return carry

    def send_later(other, carry):
        send_chip(other, (1, 3))
        return carry

    lax.fori_loop(1, CH, send_tail, 0)
    lax.fori_loop(chip + 1, CH, send_later, 0)
    for a, (src, dst) in enumerate(kv_slots(me)):
        send(src.at[:, cols(chip)], dst, send_rel.at[a, chip], recv_rel.at[a, chip], partner)

    for a in range(2):
        wait_bytes(give.at[a], local.at[6 + a])
    for h in range(NB):
        at = slice(h * BLK, (h + 1) * BLK)
        product = give[0, at, :].astype(F32) * give[1, at, :].astype(F32)
        dls[h, :, 0:BLK] = jnp.sum(product.T, axis=0, keepdims=True)
        dls[h, :, BLK:] = bit_ref[4:5, :].astype(F32)
    dlg[me] = dls[me]

    def send_peer(peer):
        send(q_ref.at[:, cols(peer)], qd.at[0, rows(me)], send_q.at[0, peer], recv_q.at[0, me], peer)
        send(do_ref.at[:, cols(peer)], qd.at[1, rows(me)], send_q.at[1, peer], recv_q.at[1, me], peer)
        send(dls.at[peer], dlg.at[me], send_l.at[peer], recv_l.at[me], peer)

    send_peer(partner)

    def send_step(step, carry):
        other = lax.rem(chip + CH - step, CH)
        for peer in (other * 2, other * 2 + 1):

            @pl.when(other < chip)
            def _():
                for a, src, dst in ((0, k_ref, ek), (1, v_ref, ev)):
                    send(src.at[:, cols(other)], dst.at[rows(NB + me)], send_s.at[a, peer], recv_s.at[a, me], peer)

            send_peer(peer)
        return carry

    lax.fori_loop(1, CH, send_step, 0)
    g[...] = jnp.zeros_like(g)

    def relay(other, kinds):
        slots = kv_slots(other * 2 + core)
        for a in kinds:
            view = slots[a][1]
            wait_bytes(view, recv_kv.at[a, other])
            send(view, view, send_rel.at[a, other], recv_rel.at[a, other], partner)

    def relay_tail(step, carry):
        relay(lax.rem(chip + CH - step, CH), (0, 2))
        return carry

    def relay_early(step, carry):
        relay(chip - step, (1, 3))
        return carry

    lax.fori_loop(1, CH, relay_tail, 0)
    lax.fori_loop(1, chip + 1, relay_early, 0)

    def arrived(other, kinds):
        slots = kv_slots(other * 2 + 1 - core)
        for a in kinds:
            wait_bytes(slots[a][1], recv_rel.at[a, other])
            wait_bytes(slots[a][1], send_rel.at[a, other])

    def arrived_tail(other, carry):
        arrived(other, (0, 2))
        return carry

    def arrived_early(other, carry):
        arrived(other, (1, 3))
        return carry

    lax.fori_loop(0, CH, arrived_tail, 0)
    lax.fori_loop(0, chip + 1, arrived_early, 0)
    for copy in own:
        copy.wait()

    def pick(read, low, high, shift):
        def block(j):
            a = [read(lax.rem(j + NB + k * shift, NB)).astype(F32) for k in range(4)]
            even = jnp.where(bits[low], a[1], a[0])
            odd = jnp.where(bits[low], a[3], a[2])
            return jnp.where(bits[high], odd, even).astype(BF)

        return block

    def near(a):
        return pick(lambda j: tails[a, rows(j), :], 0, 1, 1)

    def far(a):
        return pick(lambda j: give[a, rows(j), :], 2, 3, 4)

    def turn_near(j, carry):
        give[0, rows(j), :] = near(0)(j)
        give[1, rows(j), :] = near(1)(j)
        return carry

    def turn_far(j, carry):
        ek[rows(j), :] = far(0)(j)
        ev[rows(j), :] = far(1)(j)
        return carry

    lax.fori_loop(0, NB, turn_near, 0)
    lax.fori_loop(0, NB, turn_far, 0)

    def send_dq(tile):
        for peer in (tile * 2, tile * 2 + 1):

            @pl.when(peer != me)
            def _():
                send(dqb.at[rows(peer)], gq_ref.at[:, cols(me)], send_d.at[peer], recv_d.at[me], peer)

    def step_tile(step, carry):
        tile = lax.rem(chip + step, CH)
        for peer in (tile * 2, tile * 2 + 1):

            @pl.when(peer != me)
            def _():
                wait_bytes(qd.at[0, rows(peer)], recv_q.at[0, peer])
                wait_bytes(qd.at[1, rows(peer)], recv_q.at[1, peer])
                wait_bytes(dlg.at[peer], recv_l.at[peer])

            @pl.when(tile > chip)
            def _():
                wait_bytes(ek.at[rows(NB + peer)], recv_s.at[0, peer])
                wait_bytes(ev.at[rows(NB + peer)], recv_s.at[1, peer])

        @pl.when(step > 0)
        def _():
            send_dq(lax.rem(chip + step + CH - 1, CH))

        first = pl.multiple_of(tile * TQ, TQ)
        low = dlg[tile * 2]
        high = dlg[tile * 2 + 1]
        dl = jnp.concatenate([low[:, :BLK], high[:, :BLK]], axis=1)
        lane = lax.broadcasted_iota(jnp.int32, (1, D), 1).astype(F32)
        live = jnp.concatenate(
            [
                lane < low[:, BLK:],
                lane + D < low[:, BLK:],
                lane < high[:, BLK:],
                lane + D < high[:, BLK:],
            ],
            axis=1,
        )
        dqb[pair(tile), :] = attend(
            first, qd[0, pair(tile), :], qd[1, pair(tile), :], dl, live,
            ek, ev, g, p_s, u_s, d_s, wq, wd,
        )
        return carry

    lax.fori_loop(0, CH, step_tile, 0)

    def tile_at(step):
        return lax.rem(chip + 1 + step, CH)

    def stretch(tile):
        return pl.ds(pl.multiple_of(WIN + tile * TQ, TQ), TQ)

    def prepare(tile):
        give[1, pair(tile), :] = g[1 - core, stretch(tile), :].astype(BF)

    def exchange(tile):
        send(give.at[1, pair(tile)], theirs.at[1, pair(tile)], send_x.at[tile], recv_x.at[tile], partner)

    prepare(tile_at(0))
    send_dq(lax.rem(chip + CH - 1, CH))

    def give_step(step, carry):
        prepare(tile_at(step))
        exchange(tile_at(step - 1))
        return carry

    lax.fori_loop(1, CH, give_step, 0)
    mine = pltpu.make_async_copy(dqb.at[rows(me)], gq_ref.at[:, cols(me)], local.at[0])
    mine.start()
    give[0] = g[1 - core, 0:WIN, :].astype(BF)
    exchange(tile_at(CH - 1))

    def combine(tile):
        wait_bytes(theirs.at[1, pair(tile)], recv_x.at[tile])
        both[1, pair(tile), :] = (
            g[core, stretch(tile), :] + theirs[1, pair(tile), :].astype(F32)
        ).astype(BF)

    def ship(buffer, kind, tile):
        for peer in (tile * 2, tile * 2 + 1):

            @pl.when(peer != me)
            def _():
                send(
                    buffer.at[1, rows(peer)], gkv_ref.at[core, kind, :, cols(chip)],
                    send_g.at[kind, peer], recv_g.at[kind, me], peer,
                )

    combine(tile_at(0))
    send(give.at[0], theirs.at[0], send_x.at[CH], recv_x.at[CH], partner)

    def ship_step(step, carry):
        combine(tile_at(step))
        ship(both, 1, tile_at(step - 1))
        return carry

    lax.fori_loop(1, CH, ship_step, 0)
    last = pltpu.make_async_copy(both.at[1, rows(me)], gkv_ref.at[core, 1, :, cols(chip)], local.at[1])
    last.start()
    ship(both, 1, chip)
    wait_bytes(theirs.at[0], recv_x.at[CH])
    mine.wait()

    def free_dq(step, carry):
        peer = lax.rem(me + step, NB)
        wait_bytes(dqb.at[rows(peer)], send_d.at[peer])
        return carry

    lax.fori_loop(1, NB, free_dq, 0)
    both[0] = (g[core, 0:WIN, :] + theirs[0].astype(F32)).astype(BF)

    def back_near(j, carry):
        tails[0, rows(j), :] = pick(lambda i: both[0, rows(i), :], 0, 1, -1)(j)
        return carry

    def back_far(j, carry):
        tails[1, rows(j), :] = pick(lambda i: tails[0, rows(i), :], 2, 3, -4)(j)
        return carry

    lax.fori_loop(0, NB, back_near, 0)
    lax.fori_loop(0, NB, back_far, 0)
    tail = pltpu.make_async_copy(tails.at[1, rows(me)], gkv_ref.at[core, 0, :, cols(chip)], local.at[2])
    tail.start()

    def ship_tail(step, carry):
        ship(tails, 0, tile_at(step))
        return carry

    lax.fori_loop(0, CH, ship_tail, 0)

    def finish(step, carry):
        peer = lax.rem(me + step, NB)
        wait_bytes(qd.at[0, rows(peer)], send_q.at[0, peer])
        wait_bytes(qd.at[1, rows(peer)], send_q.at[1, peer])
        wait_bytes(dlg.at[peer], send_l.at[peer])
        wait_bytes(dqb.at[rows(peer)], recv_d.at[peer])
        for kind in range(2):
            wait_bytes(tails.at[1, rows(peer)], send_g.at[kind, peer])
            wait_bytes(tails.at[1, rows(peer)], recv_g.at[kind, peer])
        return carry

    lax.fori_loop(1, NB, finish, 0)

    def finish_tail(step, carry):
        other = lax.rem(chip + step, CH)
        for a in (0, 2):
            wait_bytes(dqb.at[rows(other)], send_kv.at[a, other])
        return carry

    def finish_later(other, carry):
        for a in (1, 3):
            wait_bytes(dqb.at[rows(other)], send_kv.at[a, other])
        return carry

    def finish_early(peer, carry):
        for a in range(2):
            wait_bytes(dqb.at[rows(peer)], send_s.at[a, peer])
        return carry

    lax.fori_loop(1, CH, finish_tail, 0)
    lax.fori_loop(chip + 1, CH, finish_later, 0)
    lax.fori_loop(0, chip * 2, finish_early, 0)

    def finish_x(tile, carry):
        wait_bytes(theirs.at[1, pair(tile)], send_x.at[tile])
        return carry

    lax.fori_loop(0, CH, finish_x, 0)
    wait_bytes(theirs.at[0], send_x.at[CH])
    last.wait()
    tail.wait()


def run(bits, q, do, fo, k, v, tk, tv):
    any_ = pl.BlockSpec(memory_space=pl.ANY)
    dma = pltpu.SemaphoreType.DMA
    vm = pltpu.VMEM
    return pl.pallas_call(
        whole,
        in_specs=[pl.BlockSpec(memory_space=pltpu.VMEM)] + [any_] * 7,
        out_specs=[any_] * 2,
        out_shape=[
            jax.ShapeDtypeStruct((BLK, NB * D), BF),
            jax.ShapeDtypeStruct((2, 2, BLK, CH * D), BF),
        ],
        scratch_shapes=[
            vm((2, WIN, D), BF), vm((NB, 1, BLK + D), F32), vm((NB, 1, BLK + D), F32),
            vm((2, WIN, D), BF),
            vm((2 * WIN, D), BF), vm((2 * WIN, D), BF), vm((2, 2 * WIN, D), F32),
            vm((WIN, TQ), F32), vm((WIN, TQ), F32), vm((WIN, TQ), F32), vm((D, TQ), BF), vm((D, TQ), BF),
            vm((2, WIN, D), BF), vm((2, WIN, D), BF),
            dma((2, NB)), dma((NB,)), dma((4, CH)), dma((4, CH)),
            dma((2, NB)), dma((NB,)), dma((4, CH)), dma((4, CH)), dma((8,)),
            dma((2, NB)), dma((2, NB)), dma((NB,)), dma((NB,)), dma((CH + 1,)), dma((CH + 1,)), dma((2, NB)), dma((2, NB)),
        ],
        compiler_params=pltpu.CompilerParams(
            collective_id=0, has_side_effects=True, vmem_limit_bytes=62 << 20
        ),
    )(bits, q, do, fo, k, v, tk, tv)


def per_device(query, keys, values, tail_keys, cached_tail_values, output_gradient, forward_output, stretch_index, valid_counts):
    powers = jnp.left_shift(1, jnp.arange(8, dtype=jnp.int32))
    rank = jnp.arange(8, dtype=jnp.int32)
    table = jnp.where(rank < 4, jnp.bitwise_and(stretch_index, powers), valid_counts)
    bits = jnp.broadcast_to(table[:, None], (8, D))
    gq, gkv = run(
        bits, query, output_gradient, forward_output, keys, values, tail_keys, cached_tail_values
    )
    return gq, gkv[0, 1], gkv[1, 1], gkv[0, 0], gkv[1, 0]


def solution(mesh):
    tokens = P(("section", "seq"), None)
    return jax.shard_map(
        per_device,
        mesh=mesh,
        in_specs=(tokens,) * 7 + (P(), P(("section", "seq"))),
        out_specs=(tokens,) * 5,
        check_vma=False,
    )
```

```python
import math

import jax
import jax.numpy as jnp
from jax import lax
from jax.experimental import pallas as pl
from jax.experimental.pallas import tpu as pltpu
from jax.sharding import PartitionSpec as P

D = 128
BLK = 256
NB = 16
CH = NB // 2
TQ = 2 * BLK
WIN = NB * BLK
SUB = 256
LONG = 1792
SCALE = 1.0 / (math.sqrt(144) * 50.0)
EXPO = 50.0 * math.log2(math.e)
F32 = jnp.float32
BF = jnp.bfloat16
MESH = pl.DeviceIdType.MESH


def to(peer):
    return {"seq": peer}


def wait_bytes(view, sem):
    pltpu.make_async_copy(view, view, sem).wait()


def cols(index):
    return pl.ds(pl.multiple_of(index * D, D), D)


def rows(index):
    return pl.ds(pl.multiple_of(index * BLK, BLK), BLK)


def pair(index):
    return pl.ds(pl.multiple_of(index * TQ, TQ), TQ)


def send(src, dst, send_sem, recv_sem, peer):
    pltpu.make_async_remote_copy(
        src_ref=src, dst_ref=dst, send_sem=send_sem, recv_sem=recv_sem,
        device_id=to(peer), device_id_type=MESH,
    ).start()


def attend(first, q, do, dl, live, ek, ev, g, p_s, u_s, d_s, wq, wd):
    wq[...] = q.T
    wd[...] = do.T

    def scores(r0, n):
        return jnp.dot(ek[pl.ds(r0, n), :], wq[...], preferred_element_type=F32) * SCALE

    def dprob(r0, n):
        return jnp.dot(ev[pl.ds(r0, n), :], wd[...], preferred_element_type=F32)

    def weigh(at, x, dp):
        n = x.shape[0]
        th = jnp.tanh(x)
        p = jnp.exp2(EXPO * th)
        p_s[at, :] = p
        u_s[at, :] = 1.0 - th * th
        d_s[at, :] = dp
        return p.reshape(n // 8, 8, TQ).sum(0)

    def older(n, start):
        row = lax.broadcasted_iota(jnp.int32, (n, TQ), 0) + start
        return row > lax.broadcasted_iota(jnp.int32, (n, TQ), 1)

    total = jnp.zeros((8, TQ), F32)
    for s in range(TQ // SUB):
        old = older(SUB, s * SUB)
        ra = pl.multiple_of(first + s * SUB, SUB)
        rb = pl.multiple_of(first + WIN + s * SUB, SUB)
        x = jnp.where(old, scores(ra, SUB), scores(rb, SUB))
        dp = jnp.where(old, dprob(ra, SUB), dprob(rb, SUB))
        total = total + weigh(pl.ds(s * SUB, SUB), x, dp)

    def forward(m, total):
        r0 = pl.multiple_of(first + TQ + m * LONG, BLK)
        at = pl.multiple_of(TQ + m * LONG, BLK)
        for s in range(LONG // SUB):
            total = total + weigh(
                pl.ds(at + s * SUB, SUB), scores(r0 + s * SUB, SUB), dprob(r0 + s * SUB, SUB)
            )
        return total

    total = lax.fori_loop(0, (WIN - TQ) // LONG, forward, total)
    inv = jnp.where(live, 1.0 / jnp.sum(total, axis=0, keepdims=True), 0.0)

    def weights(at):
        p = p_s[at, :] * inv
        return p, (p * u_s[at, :]) * ((d_s[at, :] - dl) * (1.0 / 12.0))

    def add(r0, n, p, h):
        p = p.astype(BF)
        h = h.astype(BF)
        g[1, pl.ds(r0, n), :] += jnp.dot(p, do, preferred_element_type=F32)
        g[0, pl.ds(r0, n), :] += jnp.dot(h, q, preferred_element_type=F32)
        return lax.dot_general(
            ek[pl.ds(r0, n), :], h, (((0,), (0,)), ((), ())), preferred_element_type=F32
        )

    old = older(TQ, 0)
    p, h = weights(pl.ds(0, TQ))
    zero = jnp.zeros_like(p)
    acc = add(first, TQ, jnp.where(old, p, zero), jnp.where(old, h, zero))
    acc = acc + add(first + WIN, TQ, jnp.where(old, zero, p), jnp.where(old, zero, h))

    def backward(m, acc):
        r0 = pl.multiple_of(first + TQ + m * LONG, BLK)
        at = pl.ds(pl.multiple_of(TQ + m * LONG, BLK), LONG)
        return acc + add(r0, LONG, *weights(at))

    acc = lax.fori_loop(0, (WIN - TQ) // LONG, backward, acc)
    return acc.T.astype(BF)


def whole(
    bit_ref, q_ref, do_ref, fo_ref, k_ref, v_ref, tk_ref, tv_ref,
    gq_ref, gkv_ref,
    qd, dlg, dls, tails, ek, ev, g, p_s, u_s, d_s, wq, wd, give, theirs,
    send_q, send_l, send_kv, send_rel, recv_q, recv_l, recv_kv, recv_rel, local,
    send_d, recv_d, send_x, recv_x, send_g, recv_g,
):
    me = lax.axis_index("seq")
    chip = me // 2
    core = lax.rem(me, 2)
    partner = chip * 2 + 1 - core
    dqb = tails.at[0]
    both = qd
    bits = [bit_ref[b : b + 1, :] > 0 for b in range(4)]

    def kv_slots(device):
        return (
            (tk_ref, tails.at[0, rows(device)]),
            (k_ref, ek.at[rows(NB + device)]),
            (tv_ref, tails.at[1, rows(device)]),
            (v_ref, ev.at[rows(NB + device)]),
        )

    own = [
        pltpu.make_async_copy(src.at[:, cols(chip)], dst, local.at[a])
        for a, (src, dst) in enumerate(kv_slots(me))
    ]
    own.append(pltpu.make_async_copy(q_ref.at[:, cols(me)], qd.at[0, rows(me)], local.at[4]))
    own.append(pltpu.make_async_copy(do_ref.at[:, cols(me)], qd.at[1, rows(me)], local.at[5]))

    def fetch(h, carry):
        for a, src in enumerate((do_ref, fo_ref)):
            pltpu.make_async_copy(src.at[:, cols(h)], give.at[a, rows(h)], local.at[6 + a]).start()
        return carry

    lax.fori_loop(0, NB, fetch, 0)
    for copy in own:
        copy.start()

    barrier = pltpu.get_barrier_semaphore()

    def greet(step, carry):
        pl.semaphore_signal(
            barrier, inc=1, device_id=to(lax.rem(me + step, NB)), device_id_type=MESH
        )
        return carry

    lax.fori_loop(1, NB, greet, 0)
    pl.semaphore_wait(barrier, NB - 1)

    def send_chip(other, kinds):
        slots = kv_slots(me)
        for a in kinds:
            src, dst = slots[a]
            send(src.at[:, cols(other)], dst, send_kv.at[a, other], recv_kv.at[a, chip], other * 2 + core)

    def send_all(step, carry):
        send_chip(lax.rem(chip + step, CH), range(4))
        return carry

    lax.fori_loop(1, CH, send_all, 0)
    for a, (src, dst) in enumerate(kv_slots(me)):
        send(src.at[:, cols(chip)], dst, send_rel.at[a, chip], recv_rel.at[a, chip], partner)

    for a in range(2):
        wait_bytes(give.at[a], local.at[6 + a])
    for h in range(NB):
        at = slice(h * BLK, (h + 1) * BLK)
        product = give[0, at, :].astype(F32) * give[1, at, :].astype(F32)
        dls[h, :, 0:BLK] = jnp.sum(product.T, axis=0, keepdims=True)
        dls[h, :, BLK:] = bit_ref[4:5, :].astype(F32)
    dlg[me] = dls[me]

    def send_peer(peer):
        send(q_ref.at[:, cols(peer)], qd.at[0, rows(me)], send_q.at[0, peer], recv_q.at[0, me], peer)
        send(do_ref.at[:, cols(peer)], qd.at[1, rows(me)], send_q.at[1, peer], recv_q.at[1, me], peer)
        send(dls.at[peer], dlg.at[me], send_l.at[peer], recv_l.at[me], peer)

    send_peer(partner)

    def send_step(step, carry):
        other = lax.rem(chip + CH - step, CH)
        for peer in (other * 2, other * 2 + 1):
            send_peer(peer)
        return carry

    lax.fori_loop(1, CH, send_step, 0)
    g[...] = jnp.zeros_like(g)

    def relay(other, kinds):
        slots = kv_slots(other * 2 + core)
        for a in kinds:
            view = slots[a][1]
            wait_bytes(view, recv_kv.at[a, other])
            send(view, view, send_rel.at[a, other], recv_rel.at[a, other], partner)

    def relay_all(step, carry):
        relay(lax.rem(chip + CH - step, CH), range(4))
        return carry

    lax.fori_loop(1, CH, relay_all, 0)

    def arrived(other, kinds):
        slots = kv_slots(other * 2 + 1 - core)
        for a in kinds:
            wait_bytes(slots[a][1], recv_rel.at[a, other])
            wait_bytes(slots[a][1], send_rel.at[a, other])

    def arrived_all(other, carry):
        arrived(other, range(4))
        return carry

    lax.fori_loop(0, CH, arrived_all, 0)
    for copy in own:
        copy.wait()

    def pick(read, low, high, shift):
        def block(j):
            a = [read(lax.rem(j + NB + k * shift, NB)).astype(F32) for k in range(4)]
            even = jnp.where(bits[low], a[1], a[0])
            odd = jnp.where(bits[low], a[3], a[2])
            return jnp.where(bits[high], odd, even).astype(BF)

        return block

    def near(a):
        return pick(lambda j: tails[a, rows(j), :], 0, 1, 1)

    def far(a):
        return pick(lambda j: give[a, rows(j), :], 2, 3, 4)

    def turn_near(j, carry):
        give[0, rows(j), :] = near(0)(j)
        give[1, rows(j), :] = near(1)(j)
        return carry

    def turn_far(j, carry):
        ek[rows(j), :] = far(0)(j)
        ev[rows(j), :] = far(1)(j)
        return carry

    lax.fori_loop(0, NB, turn_near, 0)
    lax.fori_loop(0, NB, turn_far, 0)

    def send_dq(tile):
        for peer in (tile * 2, tile * 2 + 1):

            @pl.when(peer != me)
            def _():
                send(dqb.at[rows(peer)], gq_ref.at[:, cols(me)], send_d.at[peer], recv_d.at[me], peer)

    def step_tile(step, carry):
        tile = lax.rem(chip + step, CH)
        for peer in (tile * 2, tile * 2 + 1):

            @pl.when(peer != me)
            def _():
                wait_bytes(qd.at[0, rows(peer)], recv_q.at[0, peer])
                wait_bytes(qd.at[1, rows(peer)], recv_q.at[1, peer])
                wait_bytes(dlg.at[peer], recv_l.at[peer])

        @pl.when(step > 0)
        def _():
            send_dq(lax.rem(chip + step + CH - 1, CH))

        first = pl.multiple_of(tile * TQ, TQ)
        low = dlg[tile * 2]
        high = dlg[tile * 2 + 1]
        dl = jnp.concatenate([low[:, :BLK], high[:, :BLK]], axis=1)
        lane = lax.broadcasted_iota(jnp.int32, (1, D), 1).astype(F32)
        live = jnp.concatenate(
            [
                lane < low[:, BLK:],
                lane + D < low[:, BLK:],
                lane < high[:, BLK:],
                lane + D < high[:, BLK:],
            ],
            axis=1,
        )
        dqb[pair(tile), :] = attend(
            first, qd[0, pair(tile), :], qd[1, pair(tile), :], dl, live,
            ek, ev, g, p_s, u_s, d_s, wq, wd,
        )
        return carry

    lax.fori_loop(0, CH, step_tile, 0)

    def tile_at(step):
        return lax.rem(chip + 1 + step, CH)

    def stretch(tile):
        return pl.ds(pl.multiple_of(WIN + tile * TQ, TQ), TQ)

    def prepare(tile):
        give[1, pair(tile), :] = g[1 - core, stretch(tile), :].astype(BF)

    def exchange(tile):
        send(give.at[1, pair(tile)], theirs.at[1, pair(tile)], send_x.at[tile], recv_x.at[tile], partner)

    prepare(tile_at(0))
    send_dq(lax.rem(chip + CH - 1, CH))

    def give_step(step, carry):
        prepare(tile_at(step))
        exchange(tile_at(step - 1))
        return carry

    lax.fori_loop(1, CH, give_step, 0)
    mine = pltpu.make_async_copy(dqb.at[rows(me)], gq_ref.at[:, cols(me)], local.at[0])
    mine.start()
    give[0] = g[1 - core, 0:WIN, :].astype(BF)
    exchange(tile_at(CH - 1))

    def combine(tile):
        wait_bytes(theirs.at[1, pair(tile)], recv_x.at[tile])
        both[1, pair(tile), :] = (
            g[core, stretch(tile), :] + theirs[1, pair(tile), :].astype(F32)
        ).astype(BF)

    def ship(buffer, kind, tile):
        for peer in (tile * 2, tile * 2 + 1):

            @pl.when(peer != me)
            def _():
                send(
                    buffer.at[1, rows(peer)], gkv_ref.at[core, kind, :, cols(chip)],
                    send_g.at[kind, peer], recv_g.at[kind, me], peer,
                )

    combine(tile_at(0))
    send(give.at[0], theirs.at[0], send_x.at[CH], recv_x.at[CH], partner)

    def ship_step(step, carry):
        combine(tile_at(step))
        ship(both, 1, tile_at(step - 1))
        return carry

    lax.fori_loop(1, CH, ship_step, 0)
    last = pltpu.make_async_copy(both.at[1, rows(me)], gkv_ref.at[core, 1, :, cols(chip)], local.at[1])
    last.start()
    ship(both, 1, chip)
    wait_bytes(theirs.at[0], recv_x.at[CH])
    mine.wait()

    def free_dq(step, carry):
        peer = lax.rem(me + step, NB)
        wait_bytes(dqb.at[rows(peer)], send_d.at[peer])
        return carry

    lax.fori_loop(1, NB, free_dq, 0)
    both[0] = (g[core, 0:WIN, :] + theirs[0].astype(F32)).astype(BF)

    def back_near(j, carry):
        tails[0, rows(j), :] = pick(lambda i: both[0, rows(i), :], 0, 1, -1)(j)
        return carry

    def back_far(j, carry):
        tails[1, rows(j), :] = pick(lambda i: tails[0, rows(i), :], 2, 3, -4)(j)
        return carry

    lax.fori_loop(0, NB, back_near, 0)
    lax.fori_loop(0, NB, back_far, 0)
    tail = pltpu.make_async_copy(tails.at[1, rows(me)], gkv_ref.at[core, 0, :, cols(chip)], local.at[2])
    tail.start()

    def ship_tail(step, carry):
        ship(tails, 0, tile_at(step))
        return carry

    lax.fori_loop(0, CH, ship_tail, 0)

    def finish(step, carry):
        peer = lax.rem(me + step, NB)
        wait_bytes(qd.at[0, rows(peer)], send_q.at[0, peer])
        wait_bytes(qd.at[1, rows(peer)], send_q.at[1, peer])
        wait_bytes(dlg.at[peer], send_l.at[peer])
        wait_bytes(dqb.at[rows(peer)], recv_d.at[peer])
        for kind in range(2):
            wait_bytes(tails.at[1, rows(peer)], send_g.at[kind, peer])
            wait_bytes(tails.at[1, rows(peer)], recv_g.at[kind, peer])
        return carry

    lax.fori_loop(1, NB, finish, 0)

    def finish_kv(step, carry):
        other = lax.rem(chip + step, CH)
        for a in range(4):
            wait_bytes(dqb.at[rows(other)], send_kv.at[a, other])
        return carry

    lax.fori_loop(1, CH, finish_kv, 0)

    def finish_x(tile, carry):
        wait_bytes(theirs.at[1, pair(tile)], send_x.at[tile])
        return carry

    lax.fori_loop(0, CH, finish_x, 0)
    wait_bytes(theirs.at[0], send_x.at[CH])
    last.wait()
    tail.wait()


def run(bits, q, do, fo, k, v, tk, tv):
    any_ = pl.BlockSpec(memory_space=pl.ANY)
    dma = pltpu.SemaphoreType.DMA
    vm = pltpu.VMEM
    return pl.pallas_call(
        whole,
        in_specs=[pl.BlockSpec(memory_space=pltpu.VMEM)] + [any_] * 7,
        out_specs=[any_] * 2,
        out_shape=[
            jax.ShapeDtypeStruct((BLK, NB * D), BF),
            jax.ShapeDtypeStruct((2, 2, BLK, CH * D), BF),
        ],
        scratch_shapes=[
            vm((2, WIN, D), BF), vm((NB, 1, BLK + D), F32), vm((NB, 1, BLK + D), F32),
            vm((2, WIN, D), BF),
            vm((2 * WIN, D), BF), vm((2 * WIN, D), BF), vm((2, 2 * WIN, D), F32),
            vm((WIN, TQ), F32), vm((WIN, TQ), F32), vm((WIN, TQ), F32), vm((D, TQ), BF), vm((D, TQ), BF),
            vm((2, WIN, D), BF), vm((2, WIN, D), BF),
            dma((2, NB)), dma((NB,)), dma((4, CH)), dma((4, CH)),
            dma((2, NB)), dma((NB,)), dma((4, CH)), dma((4, CH)), dma((8,)),
            dma((NB,)), dma((NB,)), dma((CH + 1,)), dma((CH + 1,)), dma((2, NB)), dma((2, NB)),
        ],
        compiler_params=pltpu.CompilerParams(
            collective_id=0, has_side_effects=True, vmem_limit_bytes=62 << 20
        ),
    )(bits, q, do, fo, k, v, tk, tv)


def per_device(query, keys, values, tail_keys, cached_tail_values, output_gradient, forward_output, stretch_index, valid_counts):
    powers = jnp.left_shift(1, jnp.arange(8, dtype=jnp.int32))
    rank = jnp.arange(8, dtype=jnp.int32)
    table = jnp.where(rank < 4, jnp.bitwise_and(stretch_index, powers), valid_counts)
    bits = jnp.broadcast_to(table[:, None], (8, D))
    gq, gkv = run(
        bits, query, output_gradient, forward_output, keys, values, tail_keys, cached_tail_values
    )
    return gq, gkv[0, 1], gkv[1, 1], gkv[0, 0], gkv[1, 0]


def solution(mesh):
    tokens = P(("section", "seq"), None)
    return jax.shard_map(
        per_device,
        mesh=mesh,
        in_specs=(tokens,) * 7 + (P(), P(("section", "seq"))),
        out_specs=(tokens,) * 5,
        check_vma=False,
    )
```

```python
import math

import jax
import jax.numpy as jnp
from jax import lax
from jax.experimental import pallas as pl
from jax.experimental.pallas import tpu as pltpu
from jax.sharding import PartitionSpec as P

D = 128
BLK = 256
NB = 16
CH = NB // 2
TQ = 2 * BLK
WIN = NB * BLK
SUB = 256
LONG = 1792
SCALE = 1.0 / (math.sqrt(144) * 50.0)
EXPO = 50.0 * math.log2(math.e)
F32 = jnp.float32
BF = jnp.bfloat16
MESH = pl.DeviceIdType.MESH


def to(peer):
    return {"seq": peer}


def wait_bytes(view, sem):
    pltpu.make_async_copy(view, view, sem).wait()


def cols(index):
    return pl.ds(pl.multiple_of(index * D, D), D)


def rows(index):
    return pl.ds(pl.multiple_of(index * BLK, BLK), BLK)


def pair(index):
    return pl.ds(pl.multiple_of(index * TQ, TQ), TQ)


def send(src, dst, send_sem, recv_sem, peer):
    pltpu.make_async_remote_copy(
        src_ref=src, dst_ref=dst, send_sem=send_sem, recv_sem=recv_sem,
        device_id=to(peer), device_id_type=MESH,
    ).start()


def attend(first, q, do, dl, live, ek, ev, g, p_s, u_s, d_s, wq, wd):
    wq[...] = q.T
    wd[...] = do.T

    def scores(r0, n):
        return jnp.dot(ek[pl.ds(r0, n), :], wq[...], preferred_element_type=F32) * SCALE

    def dprob(r0, n):
        return jnp.dot(ev[pl.ds(r0, n), :], wd[...], preferred_element_type=F32)

    def weigh(at, x, dp):
        n = x.shape[0]
        th = jnp.tanh(x)
        p = jnp.exp2(EXPO * th)
        p_s[at, :] = p
        u_s[at, :] = 1.0 - th * th
        d_s[at, :] = dp
        return p.reshape(n // 8, 8, TQ).sum(0)

    def older(n, start):
        row = lax.broadcasted_iota(jnp.int32, (n, TQ), 0) + start
        return row > lax.broadcasted_iota(jnp.int32, (n, TQ), 1)

    total = jnp.zeros((8, TQ), F32)
    for s in range(TQ // SUB):
        old = older(SUB, s * SUB)
        ra = pl.multiple_of(first + s * SUB, SUB)
        rb = pl.multiple_of(first + WIN + s * SUB, SUB)
        x = jnp.where(old, scores(ra, SUB), scores(rb, SUB))
        dp = jnp.where(old, dprob(ra, SUB), dprob(rb, SUB))
        total = total + weigh(pl.ds(s * SUB, SUB), x, dp)

    for m in range(TQ, WIN, SUB):
        r0 = pl.multiple_of(first + m, BLK)
        total = total + weigh(pl.ds(m, SUB), scores(r0, SUB), dprob(r0, SUB))
    inv = jnp.where(live, 1.0 / jnp.sum(total, axis=0, keepdims=True), 0.0)

    def weights(at):
        p = p_s[at, :] * inv
        return p, (p * u_s[at, :]) * ((d_s[at, :] - dl) * (1.0 / 12.0))

    def add(r0, n, p, h):
        p = p.astype(BF)
        h = h.astype(BF)
        g[1, pl.ds(r0, n), :] += jnp.dot(p, do, preferred_element_type=F32)
        g[0, pl.ds(r0, n), :] += jnp.dot(h, q, preferred_element_type=F32)
        return lax.dot_general(
            ek[pl.ds(r0, n), :], h, (((0,), (0,)), ((), ())), preferred_element_type=F32
        )

    old = older(TQ, 0)
    p, h = weights(pl.ds(0, TQ))
    zero = jnp.zeros_like(p)
    acc = add(first, TQ, jnp.where(old, p, zero), jnp.where(old, h, zero))
    acc = acc + add(first + WIN, TQ, jnp.where(old, zero, p), jnp.where(old, zero, h))

    def backward(m, acc):
        r0 = pl.multiple_of(first + TQ + m * LONG, BLK)
        at = pl.ds(pl.multiple_of(TQ + m * LONG, BLK), LONG)
        return acc + add(r0, LONG, *weights(at))

    acc = lax.fori_loop(0, (WIN - TQ) // LONG, backward, acc)
    return acc.T.astype(BF)


def whole(
    bit_ref, q_ref, do_ref, fo_ref, k_ref, v_ref, tk_ref, tv_ref,
    gq_ref, gkv_ref,
    qd, dlg, dls, tails, ek, ev, g, p_s, u_s, d_s, wq, wd, give, theirs,
    send_q, send_l, send_kv, send_rel, recv_q, recv_l, recv_kv, recv_rel, local,
    send_d, recv_d, send_x, recv_x, send_g, recv_g,
):
    me = lax.axis_index("seq")
    chip = me // 2
    core = lax.rem(me, 2)
    partner = chip * 2 + 1 - core
    dqb = tails.at[0]
    both = qd
    bits = [bit_ref[b : b + 1, :] > 0 for b in range(4)]

    def kv_slots(device):
        return (
            (tk_ref, tails.at[0, rows(device)]),
            (k_ref, ek.at[rows(NB + device)]),
            (tv_ref, tails.at[1, rows(device)]),
            (v_ref, ev.at[rows(NB + device)]),
        )

    own = [
        pltpu.make_async_copy(src.at[:, cols(chip)], dst, local.at[a])
        for a, (src, dst) in enumerate(kv_slots(me))
    ]
    own.append(pltpu.make_async_copy(q_ref.at[:, cols(me)], qd.at[0, rows(me)], local.at[4]))
    own.append(pltpu.make_async_copy(do_ref.at[:, cols(me)], qd.at[1, rows(me)], local.at[5]))

    def fetch(h, carry):
        for a, src in enumerate((do_ref, fo_ref)):
            pltpu.make_async_copy(src.at[:, cols(h)], give.at[a, rows(h)], local.at[6 + a]).start()
        return carry

    lax.fori_loop(0, NB, fetch, 0)
    for copy in own:
        copy.start()

    barrier = pltpu.get_barrier_semaphore()

    def greet(step, carry):
        pl.semaphore_signal(
            barrier, inc=1, device_id=to(lax.rem(me + step, NB)), device_id_type=MESH
        )
        return carry

    lax.fori_loop(1, NB, greet, 0)
    pl.semaphore_wait(barrier, NB - 1)

    def send_chip(other, kinds):
        slots = kv_slots(me)
        for a in kinds:
            src, dst = slots[a]
            send(src.at[:, cols(other)], dst, send_kv.at[a, other], recv_kv.at[a, chip], other * 2 + core)

    def send_all(step, carry):
        send_chip(lax.rem(chip + step, CH), range(4))
        return carry

    lax.fori_loop(1, CH, send_all, 0)
    for a, (src, dst) in enumerate(kv_slots(me)):
        send(src.at[:, cols(chip)], dst, send_rel.at[a, chip], recv_rel.at[a, chip], partner)

    for a in range(2):
        wait_bytes(give.at[a], local.at[6 + a])
    for h in range(NB):
        at = slice(h * BLK, (h + 1) * BLK)
        product = give[0, at, :].astype(F32) * give[1, at, :].astype(F32)
        dls[h, :, 0:BLK] = jnp.sum(product.T, axis=0, keepdims=True)
        dls[h, :, BLK:] = bit_ref[4:5, :].astype(F32)
    dlg[me] = dls[me]

    def send_peer(peer):
        send(q_ref.at[:, cols(peer)], qd.at[0, rows(me)], send_q.at[0, peer], recv_q.at[0, me], peer)
        send(do_ref.at[:, cols(peer)], qd.at[1, rows(me)], send_q.at[1, peer], recv_q.at[1, me], peer)
        send(dls.at[peer], dlg.at[me], send_l.at[peer], recv_l.at[me], peer)

    send_peer(partner)

    def send_step(step, carry):
        other = lax.rem(chip + CH - step, CH)
        for peer in (other * 2, other * 2 + 1):
            send_peer(peer)
        return carry

    lax.fori_loop(1, CH, send_step, 0)
    g[...] = jnp.zeros_like(g)

    def relay(other, kinds):
        slots = kv_slots(other * 2 + core)
        for a in kinds:
            view = slots[a][1]
            wait_bytes(view, recv_kv.at[a, other])
            send(view, view, send_rel.at[a, other], recv_rel.at[a, other], partner)

    def relay_all(step, carry):
        relay(lax.rem(chip + CH - step, CH), range(4))
        return carry

    lax.fori_loop(1, CH, relay_all, 0)

    def arrived(other, kinds):
        slots = kv_slots(other * 2 + 1 - core)
        for a in kinds:
            wait_bytes(slots[a][1], recv_rel.at[a, other])
            wait_bytes(slots[a][1], send_rel.at[a, other])

    def arrived_all(other, carry):
        arrived(other, range(4))
        return carry

    lax.fori_loop(0, CH, arrived_all, 0)
    for copy in own:
        copy.wait()

    def pick(read, low, high, shift):
        def block(j):
            a = [read(lax.rem(j + NB + k * shift, NB)).astype(F32) for k in range(4)]
            even = jnp.where(bits[low], a[1], a[0])
            odd = jnp.where(bits[low], a[3], a[2])
            return jnp.where(bits[high], odd, even).astype(BF)

        return block

    def near(a):
        return pick(lambda j: tails[a, rows(j), :], 0, 1, 1)

    def far(a):
        return pick(lambda j: give[a, rows(j), :], 2, 3, 4)

    def turn_near(j, carry):
        give[0, rows(j), :] = near(0)(j)
        give[1, rows(j), :] = near(1)(j)
        return carry

    def turn_far(j, carry):
        ek[rows(j), :] = far(0)(j)
        ev[rows(j), :] = far(1)(j)
        return carry

    lax.fori_loop(0, NB, turn_near, 0)
    lax.fori_loop(0, NB, turn_far, 0)

    def send_dq(tile):
        for peer in (tile * 2, tile * 2 + 1):

            @pl.when(peer != me)
            def _():
                send(dqb.at[rows(peer)], gq_ref.at[:, cols(me)], send_d.at[peer], recv_d.at[me], peer)

    def step_tile(step, carry):
        tile = lax.rem(chip + step, CH)
        for peer in (tile * 2, tile * 2 + 1):

            @pl.when(peer != me)
            def _():
                wait_bytes(qd.at[0, rows(peer)], recv_q.at[0, peer])
                wait_bytes(qd.at[1, rows(peer)], recv_q.at[1, peer])
                wait_bytes(dlg.at[peer], recv_l.at[peer])

        @pl.when(step > 0)
        def _():
            send_dq(lax.rem(chip + step + CH - 1, CH))

        first = pl.multiple_of(tile * TQ, TQ)
        low = dlg[tile * 2]
        high = dlg[tile * 2 + 1]
        dl = jnp.concatenate([low[:, :BLK], high[:, :BLK]], axis=1)
        lane = lax.broadcasted_iota(jnp.int32, (1, D), 1).astype(F32)
        live = jnp.concatenate(
            [
                lane < low[:, BLK:],
                lane + D < low[:, BLK:],
                lane < high[:, BLK:],
                lane + D < high[:, BLK:],
            ],
            axis=1,
        )
        dqb[pair(tile), :] = attend(
            first, qd[0, pair(tile), :], qd[1, pair(tile), :], dl, live,
            ek, ev, g, p_s, u_s, d_s, wq, wd,
        )
        return carry

    lax.fori_loop(0, CH, step_tile, 0)

    def tile_at(step):
        return lax.rem(chip + 1 + step, CH)

    def stretch(tile):
        return pl.ds(pl.multiple_of(WIN + tile * TQ, TQ), TQ)

    def prepare(tile):
        give[1, pair(tile), :] = g[1 - core, stretch(tile), :].astype(BF)

    def exchange(tile):
        send(give.at[1, pair(tile)], theirs.at[1, pair(tile)], send_x.at[tile], recv_x.at[tile], partner)

    prepare(tile_at(0))
    send_dq(lax.rem(chip + CH - 1, CH))

    def give_step(step, carry):
        prepare(tile_at(step))
        exchange(tile_at(step - 1))
        return carry

    lax.fori_loop(1, CH, give_step, 0)
    mine = pltpu.make_async_copy(dqb.at[rows(me)], gq_ref.at[:, cols(me)], local.at[0])
    mine.start()
    give[0] = g[1 - core, 0:WIN, :].astype(BF)
    exchange(tile_at(CH - 1))

    def combine(tile):
        wait_bytes(theirs.at[1, pair(tile)], recv_x.at[tile])
        both[1, pair(tile), :] = (
            g[core, stretch(tile), :] + theirs[1, pair(tile), :].astype(F32)
        ).astype(BF)

    def ship(buffer, kind, tile):
        for peer in (tile * 2, tile * 2 + 1):

            @pl.when(peer != me)
            def _():
                send(
                    buffer.at[1, rows(peer)], gkv_ref.at[core, kind, :, cols(chip)],
                    send_g.at[kind, peer], recv_g.at[kind, me], peer,
                )

    combine(tile_at(0))
    send(give.at[0], theirs.at[0], send_x.at[CH], recv_x.at[CH], partner)

    def ship_step(step, carry):
        combine(tile_at(step))
        ship(both, 1, tile_at(step - 1))
        return carry

    lax.fori_loop(1, CH, ship_step, 0)
    last = pltpu.make_async_copy(both.at[1, rows(me)], gkv_ref.at[core, 1, :, cols(chip)], local.at[1])
    last.start()
    ship(both, 1, chip)
    wait_bytes(theirs.at[0], recv_x.at[CH])
    mine.wait()

    def free_dq(step, carry):
        peer = lax.rem(me + step, NB)
        wait_bytes(dqb.at[rows(peer)], send_d.at[peer])
        return carry

    lax.fori_loop(1, NB, free_dq, 0)
    both[0] = (g[core, 0:WIN, :] + theirs[0].astype(F32)).astype(BF)

    def back_near(j, carry):
        tails[0, rows(j), :] = pick(lambda i: both[0, rows(i), :], 0, 1, -1)(j)
        return carry

    def back_far(j, carry):
        tails[1, rows(j), :] = pick(lambda i: tails[0, rows(i), :], 2, 3, -4)(j)
        return carry

    lax.fori_loop(0, NB, back_near, 0)
    lax.fori_loop(0, NB, back_far, 0)
    tail = pltpu.make_async_copy(tails.at[1, rows(me)], gkv_ref.at[core, 0, :, cols(chip)], local.at[2])
    tail.start()

    def ship_tail(step, carry):
        ship(tails, 0, tile_at(step))
        return carry

    lax.fori_loop(0, CH, ship_tail, 0)

    def finish(step, carry):
        peer = lax.rem(me + step, NB)
        wait_bytes(qd.at[0, rows(peer)], send_q.at[0, peer])
        wait_bytes(qd.at[1, rows(peer)], send_q.at[1, peer])
        wait_bytes(dlg.at[peer], send_l.at[peer])
        wait_bytes(dqb.at[rows(peer)], recv_d.at[peer])
        for kind in range(2):
            wait_bytes(tails.at[1, rows(peer)], send_g.at[kind, peer])
            wait_bytes(tails.at[1, rows(peer)], recv_g.at[kind, peer])
        return carry

    lax.fori_loop(1, NB, finish, 0)

    def finish_kv(step, carry):
        other = lax.rem(chip + step, CH)
        for a in range(4):
            wait_bytes(dqb.at[rows(other)], send_kv.at[a, other])
        return carry

    lax.fori_loop(1, CH, finish_kv, 0)

    def finish_x(tile, carry):
        wait_bytes(theirs.at[1, pair(tile)], send_x.at[tile])
        return carry

    lax.fori_loop(0, CH, finish_x, 0)
    wait_bytes(theirs.at[0], send_x.at[CH])
    last.wait()
    tail.wait()


def run(bits, q, do, fo, k, v, tk, tv):
    any_ = pl.BlockSpec(memory_space=pl.ANY)
    dma = pltpu.SemaphoreType.DMA
    vm = pltpu.VMEM
    return pl.pallas_call(
        whole,
        in_specs=[pl.BlockSpec(memory_space=pltpu.VMEM)] + [any_] * 7,
        out_specs=[any_] * 2,
        out_shape=[
            jax.ShapeDtypeStruct((BLK, NB * D), BF),
            jax.ShapeDtypeStruct((2, 2, BLK, CH * D), BF),
        ],
        scratch_shapes=[
            vm((2, WIN, D), BF), vm((NB, 1, BLK + D), F32), vm((NB, 1, BLK + D), F32),
            vm((2, WIN, D), BF),
            vm((2 * WIN, D), BF), vm((2 * WIN, D), BF), vm((2, 2 * WIN, D), F32),
            vm((WIN, TQ), F32), vm((WIN, TQ), F32), vm((WIN, TQ), F32), vm((D, TQ), BF), vm((D, TQ), BF),
            vm((2, WIN, D), BF), vm((2, WIN, D), BF),
            dma((2, NB)), dma((NB,)), dma((4, CH)), dma((4, CH)),
            dma((2, NB)), dma((NB,)), dma((4, CH)), dma((4, CH)), dma((8,)),
            dma((NB,)), dma((NB,)), dma((CH + 1,)), dma((CH + 1,)), dma((2, NB)), dma((2, NB)),
        ],
        compiler_params=pltpu.CompilerParams(
            collective_id=0, has_side_effects=True, vmem_limit_bytes=62 << 20
        ),
    )(bits, q, do, fo, k, v, tk, tv)


def per_device(query, keys, values, tail_keys, cached_tail_values, output_gradient, forward_output, stretch_index, valid_counts):
    powers = jnp.left_shift(1, jnp.arange(8, dtype=jnp.int32))
    rank = jnp.arange(8, dtype=jnp.int32)
    table = jnp.where(rank < 4, jnp.bitwise_and(stretch_index, powers), valid_counts)
    bits = jnp.broadcast_to(table[:, None], (8, D))
    gq, gkv = run(
        bits, query, output_gradient, forward_output, keys, values, tail_keys, cached_tail_values
    )
    return gq, gkv[0, 1], gkv[1, 1], gkv[0, 0], gkv[1, 0]


def solution(mesh):
    tokens = P(("section", "seq"), None)
    return jax.shard_map(
        per_device,
        mesh=mesh,
        in_specs=(tokens,) * 7 + (P(), P(("section", "seq"))),
        out_specs=(tokens,) * 5,
        check_vma=False,
    )
```

```python
import math

import jax
import jax.numpy as jnp
from jax import lax
from jax.experimental import pallas as pl
from jax.experimental.pallas import tpu as pltpu
from jax.sharding import PartitionSpec as P

D = 128
BLK = 256
NB = 16
CH = NB // 2
TQ = 2 * BLK
WIN = NB * BLK
SUB = 256
LONG = 1792
SCALE = 1.0 / (math.sqrt(144) * 50.0)
EXPO = 50.0 * math.log2(math.e)
F32 = jnp.float32
BF = jnp.bfloat16
MESH = pl.DeviceIdType.MESH


def to(peer):
    return {"seq": peer}


def wait_bytes(view, sem):
    pltpu.make_async_copy(view, view, sem).wait()


def cols(index):
    return pl.ds(pl.multiple_of(index * D, D), D)


def rows(index):
    return pl.ds(pl.multiple_of(index * BLK, BLK), BLK)


def pair(index):
    return pl.ds(pl.multiple_of(index * TQ, TQ), TQ)


def send(src, dst, send_sem, recv_sem, peer):
    pltpu.make_async_remote_copy(
        src_ref=src, dst_ref=dst, send_sem=send_sem, recv_sem=recv_sem,
        device_id=to(peer), device_id_type=MESH,
    ).start()


def attend(first, q, do, dl, live, ek, ev, g, p_s, u_s, d_s, wq, wd):
    wq[...] = q.T
    wd[...] = do.T

    def scores(r0, n):
        return jnp.dot(ek[pl.ds(r0, n), :], wq[...], preferred_element_type=F32) * SCALE

    def dprob(r0, n):
        return jnp.dot(ev[pl.ds(r0, n), :], wd[...], preferred_element_type=F32)

    def weigh(at, x, dp):
        n = x.shape[0]
        th = jnp.tanh(x)
        p = jnp.exp2(EXPO * th)
        p_s[at, :] = p
        u_s[at, :] = 1.0 - th * th
        d_s[at, :] = dp
        return p.reshape(n // 8, 8, TQ).sum(0)

    def older(n, start):
        row = lax.broadcasted_iota(jnp.int32, (n, TQ), 0) + start
        return row > lax.broadcasted_iota(jnp.int32, (n, TQ), 1)

    total = jnp.zeros((8, TQ), F32)
    for s in range(TQ // SUB):
        old = older(SUB, s * SUB)
        ra = pl.multiple_of(first + s * SUB, SUB)
        rb = pl.multiple_of(first + WIN + s * SUB, SUB)
        x = jnp.where(old, scores(ra, SUB), scores(rb, SUB))
        dp = jnp.where(old, dprob(ra, SUB), dprob(rb, SUB))
        total = total + weigh(pl.ds(s * SUB, SUB), x, dp)

    for m in range(TQ, WIN, SUB):
        r0 = pl.multiple_of(first + m, BLK)
        total = total + weigh(pl.ds(m, SUB), scores(r0, SUB), dprob(r0, SUB))
    inv = jnp.where(live, 1.0 / jnp.sum(total, axis=0, keepdims=True), 0.0)

    def weights(at):
        p = p_s[at, :] * inv
        return p, (p * u_s[at, :]) * ((d_s[at, :] - dl) * (1.0 / 12.0))

    def add(r0, n, p, h):
        p = p.astype(BF)
        h = h.astype(BF)
        g[1, pl.ds(r0, n), :] += jnp.dot(p, do, preferred_element_type=F32)
        g[0, pl.ds(r0, n), :] += jnp.dot(h, q, preferred_element_type=F32)
        return lax.dot_general(
            ek[pl.ds(r0, n), :], h, (((0,), (0,)), ((), ())), preferred_element_type=F32
        )

    old = older(TQ, 0)
    p, h = weights(pl.ds(0, TQ))
    zero = jnp.zeros_like(p)
    acc = add(first, TQ, jnp.where(old, p, zero), jnp.where(old, h, zero))
    acc = acc + add(first + WIN, TQ, jnp.where(old, zero, p), jnp.where(old, zero, h))

    def backward(m, acc):
        r0 = pl.multiple_of(first + TQ + m * LONG, BLK)
        at = pl.ds(pl.multiple_of(TQ + m * LONG, BLK), LONG)
        return acc + add(r0, LONG, *weights(at))

    acc = lax.fori_loop(0, (WIN - TQ) // LONG, backward, acc)
    return acc.T.astype(BF)


def whole(
    bit_ref, q_ref, do_ref, fo_ref, k_ref, v_ref, tk_ref, tv_ref,
    gq_ref, gkv_ref,
    qd, dlg, dls, tails, ek, ev, g, p_s, u_s, d_s, wq, wd, give, theirs,
    send_q, send_l, send_kv, send_rel, recv_q, recv_l, recv_kv, recv_rel, local,
    send_d, recv_d, send_x, recv_x, send_g, recv_g,
):
    me = lax.axis_index("seq")
    chip = me // 2
    core = lax.rem(me, 2)
    partner = chip * 2 + 1 - core
    dqb = tails.at[0]
    both = qd
    bits = [bit_ref[b : b + 1, :] > 0 for b in range(4)]

    def kv_slots(device):
        return (
            (tk_ref, tails.at[0, rows(device)]),
            (k_ref, ek.at[rows(NB + device)]),
            (tv_ref, tails.at[1, rows(device)]),
            (v_ref, ev.at[rows(NB + device)]),
        )

    own = [
        pltpu.make_async_copy(src.at[:, cols(chip)], dst, local.at[a])
        for a, (src, dst) in enumerate(kv_slots(me))
    ]
    own.append(pltpu.make_async_copy(q_ref.at[:, cols(me)], qd.at[0, rows(me)], local.at[4]))
    own.append(pltpu.make_async_copy(do_ref.at[:, cols(me)], qd.at[1, rows(me)], local.at[5]))

    def fetch(h, carry):
        for a, src in enumerate((do_ref, fo_ref)):
            pltpu.make_async_copy(src.at[:, cols(h)], give.at[a, rows(h)], local.at[6 + a]).start()
        return carry

    lax.fori_loop(0, NB, fetch, 0)
    for copy in own:
        copy.start()

    barrier = pltpu.get_barrier_semaphore()

    def greet(step, carry):
        pl.semaphore_signal(
            barrier, inc=1, device_id=to(lax.rem(me + step, NB)), device_id_type=MESH
        )
        return carry

    lax.fori_loop(1, NB, greet, 0)
    pl.semaphore_wait(barrier, NB - 1)

    def send_chip(other, kinds):
        slots = kv_slots(me)
        for a in kinds:
            src, dst = slots[a]
            send(src.at[:, cols(other)], dst, send_kv.at[a, other], recv_kv.at[a, chip], other * 2 + core)

    def send_all(step, carry):
        send_chip(lax.rem(chip + step, CH), range(4))
        return carry

    lax.fori_loop(1, CH, send_all, 0)
    for a, (src, dst) in enumerate(kv_slots(me)):
        send(src.at[:, cols(chip)], dst, send_rel.at[a, chip], recv_rel.at[a, chip], partner)

    for a in range(2):
        wait_bytes(give.at[a], local.at[6 + a])
    for h in range(NB):
        at = slice(h * BLK, (h + 1) * BLK)
        product = give[0, at, :].astype(F32) * give[1, at, :].astype(F32)
        dls[h, :, 0:BLK] = jnp.sum(product.T, axis=0, keepdims=True)
        dls[h, :, BLK:] = bit_ref[4:5, :].astype(F32)
    dlg[me] = dls[me]

    def send_peer(peer):
        send(q_ref.at[:, cols(peer)], qd.at[0, rows(me)], send_q.at[0, peer], recv_q.at[0, me], peer)
        send(do_ref.at[:, cols(peer)], qd.at[1, rows(me)], send_q.at[1, peer], recv_q.at[1, me], peer)
        send(dls.at[peer], dlg.at[me], send_l.at[peer], recv_l.at[me], peer)

    send_peer(partner)

    def send_step(step, carry):
        other = lax.rem(chip + CH - step, CH)
        for peer in (other * 2, other * 2 + 1):
            send_peer(peer)
        return carry

    lax.fori_loop(1, CH, send_step, 0)
    g[...] = jnp.zeros_like(g)

    def relay(other, kinds):
        slots = kv_slots(other * 2 + core)
        for a in kinds:
            view = slots[a][1]
            wait_bytes(view, recv_kv.at[a, other])
            send(view, view, send_rel.at[a, other], recv_rel.at[a, other], partner)

    def relay_all(step, carry):
        relay(lax.rem(chip + CH - step, CH), range(4))
        return carry

    lax.fori_loop(1, CH, relay_all, 0)

    def arrived(other, kinds):
        slots = kv_slots(other * 2 + 1 - core)
        for a in kinds:
            wait_bytes(slots[a][1], recv_rel.at[a, other])
            wait_bytes(slots[a][1], send_rel.at[a, other])

    def arrived_all(other, carry):
        arrived(other, range(4))
        return carry

    lax.fori_loop(0, CH, arrived_all, 0)
    for copy in own:
        copy.wait()

    def pick(read, low, high, shift):
        def block(j):
            a = [read(lax.rem(j + NB + k * shift, NB)).astype(F32) for k in range(4)]
            even = jnp.where(bits[low], a[1], a[0])
            odd = jnp.where(bits[low], a[3], a[2])
            return jnp.where(bits[high], odd, even).astype(BF)

        return block

    def near(a):
        return pick(lambda j: tails[a, rows(j), :], 0, 1, 1)

    def far(a):
        return pick(lambda j: give[a, rows(j), :], 2, 3, 4)

    def turn_near(j, carry):
        give[0, rows(j), :] = near(0)(j)
        give[1, rows(j), :] = near(1)(j)
        return carry

    def turn_far(j, carry):
        ek[rows(j), :] = far(0)(j)
        ev[rows(j), :] = far(1)(j)
        return carry

    lax.fori_loop(0, NB, turn_near, 0)
    lax.fori_loop(0, NB, turn_far, 0)

    def send_dq(tile):
        for peer in (tile * 2, tile * 2 + 1):

            @pl.when(peer != me)
            def _():
                send(dqb.at[rows(peer)], gq_ref.at[:, cols(me)], send_d.at[peer], recv_d.at[me], peer)

    def stretch(tile):
        return pl.ds(pl.multiple_of(WIN + tile * TQ, TQ), TQ)

    def prepare(tile):
        give[1, pair(tile), :] = g[1 - core, stretch(tile), :].astype(BF)

    def exchange(tile):
        send(give.at[1, pair(tile)], theirs.at[1, pair(tile)], send_x.at[tile], recv_x.at[tile], partner)

    def combine(tile):
        wait_bytes(theirs.at[1, pair(tile)], recv_x.at[tile])
        both[1, pair(tile), :] = (
            g[core, stretch(tile), :] + theirs[1, pair(tile), :].astype(F32)
        ).astype(BF)

    def ship(buffer, kind, tile):
        for peer in (tile * 2, tile * 2 + 1):

            @pl.when(peer != me)
            def _():
                send(
                    buffer.at[1, rows(peer)], gkv_ref.at[core, kind, :, cols(chip)],
                    send_g.at[kind, peer], recv_g.at[kind, me], peer,
                )

    def prepare_done(b, carry):
        prepare(b)
        return carry

    def exchange_done(b, carry):
        exchange(b)
        return carry

    def combine_done(b, carry):
        combine(b)
        return carry

    def ship_done(b, carry):
        ship(both, 1, b)
        return carry

    def step_tile(step, carry):
        tile = lax.rem(chip + step, CH)
        for peer in (tile * 2, tile * 2 + 1):

            @pl.when(peer != me)
            def _():
                wait_bytes(qd.at[0, rows(peer)], recv_q.at[0, peer])
                wait_bytes(qd.at[1, rows(peer)], recv_q.at[1, peer])
                wait_bytes(dlg.at[peer], recv_l.at[peer])

        @pl.when(step > 0)
        def _():
            send_dq(lax.rem(chip + step + CH - 1, CH))

        @pl.when(jnp.logical_and(tile == 0, chip > 0))
        def _():
            lax.fori_loop(chip, CH, prepare_done, 0)
            lax.fori_loop(chip, CH, exchange_done, 0)

        @pl.when(jnp.logical_and(tile == 1, chip > 1))
        def _():
            lax.fori_loop(chip, CH, combine_done, 0)
            lax.fori_loop(chip, CH, ship_done, 0)

        first = pl.multiple_of(tile * TQ, TQ)
        low = dlg[tile * 2]
        high = dlg[tile * 2 + 1]
        dl = jnp.concatenate([low[:, :BLK], high[:, :BLK]], axis=1)
        lane = lax.broadcasted_iota(jnp.int32, (1, D), 1).astype(F32)
        live = jnp.concatenate(
            [
                lane < low[:, BLK:],
                lane + D < low[:, BLK:],
                lane < high[:, BLK:],
                lane + D < high[:, BLK:],
            ],
            axis=1,
        )
        dqb[pair(tile), :] = attend(
            first, qd[0, pair(tile), :], qd[1, pair(tile), :], dl, live,
            ek, ev, g, p_s, u_s, d_s, wq, wd,
        )
        return carry

    lax.fori_loop(0, CH, step_tile, 0)

    left_x = jnp.where(chip == 0, CH, chip)
    left_c = jnp.where(chip > 1, chip, CH)
    prepare(left_x - 1)
    send_dq(lax.rem(chip + CH - 1, CH))

    def give_step(step, carry):
        prepare(left_x - 1 - step)
        exchange(left_x - step)
        return carry

    lax.fori_loop(1, left_x, give_step, 0)
    mine = pltpu.make_async_copy(dqb.at[rows(me)], gq_ref.at[:, cols(me)], local.at[0])
    mine.start()
    give[0] = g[1 - core, 0:WIN, :].astype(BF)
    exchange(0)

    combine(left_c - 1)
    send(give.at[0], theirs.at[0], send_x.at[CH], recv_x.at[CH], partner)

    def ship_step(step, carry):
        combine(left_c - 1 - step)
        ship(both, 1, left_c - step)
        return carry

    lax.fori_loop(1, left_c, ship_step, 0)
    last = pltpu.make_async_copy(both.at[1, rows(me)], gkv_ref.at[core, 1, :, cols(chip)], local.at[1])
    last.start()
    ship(both, 1, 0)
    wait_bytes(theirs.at[0], recv_x.at[CH])
    mine.wait()

    def free_dq(step, carry):
        peer = lax.rem(me + step, NB)
        wait_bytes(dqb.at[rows(peer)], send_d.at[peer])
        return carry

    lax.fori_loop(1, NB, free_dq, 0)
    both[0] = (g[core, 0:WIN, :] + theirs[0].astype(F32)).astype(BF)

    def back_near(j, carry):
        tails[0, rows(j), :] = pick(lambda i: both[0, rows(i), :], 0, 1, -1)(j)
        return carry

    def back_far(j, carry):
        tails[1, rows(j), :] = pick(lambda i: tails[0, rows(i), :], 2, 3, -4)(j)
        return carry

    lax.fori_loop(0, NB, back_near, 0)
    lax.fori_loop(0, NB, back_far, 0)
    tail = pltpu.make_async_copy(tails.at[1, rows(me)], gkv_ref.at[core, 0, :, cols(chip)], local.at[2])
    tail.start()

    def ship_tail(step, carry):
        ship(tails, 0, lax.rem(chip + 1 + step, CH))
        return carry

    lax.fori_loop(0, CH, ship_tail, 0)

    def finish(step, carry):
        peer = lax.rem(me + step, NB)
        wait_bytes(qd.at[0, rows(peer)], send_q.at[0, peer])
        wait_bytes(qd.at[1, rows(peer)], send_q.at[1, peer])
        wait_bytes(dlg.at[peer], send_l.at[peer])
        wait_bytes(dqb.at[rows(peer)], recv_d.at[peer])
        for kind in range(2):
            wait_bytes(tails.at[1, rows(peer)], send_g.at[kind, peer])
            wait_bytes(tails.at[1, rows(peer)], recv_g.at[kind, peer])
        return carry

    lax.fori_loop(1, NB, finish, 0)

    def finish_kv(step, carry):
        other = lax.rem(chip + step, CH)
        for a in range(4):
            wait_bytes(dqb.at[rows(other)], send_kv.at[a, other])
        return carry

    lax.fori_loop(1, CH, finish_kv, 0)

    def finish_x(tile, carry):
        wait_bytes(theirs.at[1, pair(tile)], send_x.at[tile])
        return carry

    lax.fori_loop(0, CH, finish_x, 0)
    wait_bytes(theirs.at[0], send_x.at[CH])
    last.wait()
    tail.wait()


def run(bits, q, do, fo, k, v, tk, tv):
    any_ = pl.BlockSpec(memory_space=pl.ANY)
    dma = pltpu.SemaphoreType.DMA
    vm = pltpu.VMEM
    return pl.pallas_call(
        whole,
        in_specs=[pl.BlockSpec(memory_space=pltpu.VMEM)] + [any_] * 7,
        out_specs=[any_] * 2,
        out_shape=[
            jax.ShapeDtypeStruct((BLK, NB * D), BF),
            jax.ShapeDtypeStruct((2, 2, BLK, CH * D), BF),
        ],
        scratch_shapes=[
            vm((2, WIN, D), BF), vm((NB, 1, BLK + D), F32), vm((NB, 1, BLK + D), F32),
            vm((2, WIN, D), BF),
            vm((2 * WIN, D), BF), vm((2 * WIN, D), BF), vm((2, 2 * WIN, D), F32),
            vm((WIN, TQ), F32), vm((WIN, TQ), F32), vm((WIN, TQ), F32), vm((D, TQ), BF), vm((D, TQ), BF),
            vm((2, WIN, D), BF), vm((2, WIN, D), BF),
            dma((2, NB)), dma((NB,)), dma((4, CH)), dma((4, CH)),
            dma((2, NB)), dma((NB,)), dma((4, CH)), dma((4, CH)), dma((8,)),
            dma((NB,)), dma((NB,)), dma((CH + 1,)), dma((CH + 1,)), dma((2, NB)), dma((2, NB)),
        ],
        compiler_params=pltpu.CompilerParams(
            collective_id=0, has_side_effects=True, vmem_limit_bytes=62 << 20
        ),
    )(bits, q, do, fo, k, v, tk, tv)


def per_device(query, keys, values, tail_keys, cached_tail_values, output_gradient, forward_output, stretch_index, valid_counts):
    powers = jnp.left_shift(1, jnp.arange(8, dtype=jnp.int32))
    rank = jnp.arange(8, dtype=jnp.int32)
    table = jnp.where(rank < 4, jnp.bitwise_and(stretch_index, powers), valid_counts)
    bits = jnp.broadcast_to(table[:, None], (8, D))
    gq, gkv = run(
        bits, query, output_gradient, forward_output, keys, values, tail_keys, cached_tail_values
    )
    return gq, gkv[0, 1], gkv[1, 1], gkv[0, 0], gkv[1, 0]


def solution(mesh):
    tokens = P(("section", "seq"), None)
    return jax.shard_map(
        per_device,
        mesh=mesh,
        in_specs=(tokens,) * 7 + (P(), P(("section", "seq"))),
        out_specs=(tokens,) * 5,
        check_vma=False,
    )
```
